256 devices in a mesh: video: 8 (over x, y_hi), context: 32 (over y_lo, z, core).
Axes of the slice: x: 4, y: 4 (y_hi: 2, y_lo: 2; y = y_hi * 2 + y_lo), z: 8, core: 2. Of those that a mesh axis runs over, the one named last changes fastest.
Arguments:
- queries: bfloat16 [32768, 4096], P(('video', 'context')), parts along dimension 0, may hold values from -135 to 135
- keys: bfloat16 [32768, 4096], P(('video', 'context')), parts along dimension 0, may hold values from -5 to 5
- values: bfloat16 [32768, 4096], P(('video', 'context')), parts along dimension 0, may hold values from -6 to 6
- value_layer_input: bfloat16 [32768, 4096], P(('video', 'context')), parts along dimension 0, may hold values from -6 to 6
- adapter_down_weight: bfloat16 [4096, 64], replicated, may hold values from -0.09375 to 0.09375
- adapter_up_weight: bfloat16 [4096, 64], replicated, may hold values from -0.75 to 0.75
- neighbors: int32 [512, 4], P(('video', 'context')), parts along dimension 0, may hold values from 0 to 63, as said below
Outputs:
- student_out: bfloat16 [32768, 4096], P(('video', 'context')), parts along dimension 0
- grad_down: float32 [32768, 64], P(('video', 'context')), parts along dimension 0
- grad_up: float32 [32768, 64], P(('video', 'context')), parts along dimension 0
The draws below stay inside these ranges and needn't reach their ends.
There are 8 independent parts, one for each index of `video`. The reference program is written for one: setup_inputs(seed, part) draws one part's arguments, and reference() takes and returns one part's arrays. A program takes and returns all parts, laid end to end along the dimension named above; an argument that names none is the same for every part. Nothing has to cross between parts.
Inputs may be any that keep to these rules, and one draw needn't show every extreme that they name: `neighbors`: row i begins with i itself; its 4 entries are distinct tiles of the slab of tile i, the slab before or the slab after, where slab = tile // 2.
All inputs are finite; a program needn't handle non-finite values.
Results may differ from the reference program's by a relative error of at most 0.008.
Values may be sent and summed in bfloat16 or wider, within the bound.
A program may use at most 64 MiB of HBM per device.

```python
import jax
import jax.numpy as jnp
from jax import lax

H = 32
HD = 128
MODEL_WIDTH = 4096
ADAPTER_RANK = 64
TOK_DEV = 128
TILE = 64
NB = 4
TOKENS = 4096
TPD = 2
NTILES = 64
N_CONTEXT = 32


def drawn_pair(key):
    query_key = jax.random.fold_in(key, 101)
    key_key = jax.random.fold_in(key, 202)
    keys = jax.random.truncated_normal(key_key, -5.0, 5.0, (TOKENS, MODEL_WIDTH), jnp.float32)
    queries = jax.random.truncated_normal(query_key, -5.0, 5.0, (TOKENS, MODEL_WIDTH), jnp.float32)
    return (queries, keys)


def draw_queries(key, part):
    return drawn_pair(key)[0].astype(jnp.bfloat16)


def draw_keys(key, part):
    return drawn_pair(key)[1].astype(jnp.bfloat16)


def draw_neighbors(key, part):
    tiles = jnp.arange(NTILES, dtype=jnp.int32)
    slots = jnp.arange(3 * TPD, dtype=jnp.int32)
    candidates = (tiles[:, None] // TPD - 1) * TPD + slots[None, :]
    valid = (candidates >= 0) & (candidates < NTILES)
    itself = candidates == tiles[:, None]
    scores = jax.random.randint(jax.random.fold_in(key, 404), (NTILES, 3 * TPD), 0, 1000) * (3 * TPD) + slots[None, :]
    scores = jnp.where(itself, 1000000, jnp.where(valid, scores, -1 - slots[None, :]))
    order = lax.top_k(scores, NB)[1]
    return jnp.take_along_axis(candidates, order, axis=1).astype(jnp.int32)


def block_scale(rng, shape, cuts, smallest, high):
    factor_of, own = 1.0, jax.random.fold_in(rng, 6)
    for position, parts in cuts:
        draws = jnp.exp(jax.random.uniform(jax.random.fold_in(own, position), (parts,), jnp.float32, smallest / len(cuts), high / len(cuts)))
        factor_of = factor_of * jnp.repeat(draws, shape[position] // parts).reshape([-1 if axis == position else 1 for axis in range(len(shape))])
    return factor_of


def scatter_about(own_key, shape, spread, bound, pieces=(), kind=jnp.bfloat16):
    loudness = block_scale(own_key, shape, pieces, -0.22, 0.18) if pieces else 1.0
    drawn = jax.random.normal(own_key, shape, jnp.float32) * spread * loudness
    return jnp.minimum(jnp.maximum(drawn, -bound), bound).astype(kind)


def setup_inputs(seed: int = 0, part: int = 0) -> dict:
    key_list = jax.random.split(jax.random.key(seed), 8)
    own_keys = jax.random.split(jax.random.fold_in(key_list[7], part), 8)
    queries = draw_queries(jax.random.fold_in(jax.random.fold_in(key_list[7], part), 71), part)
    keys = draw_keys(jax.random.fold_in(jax.random.fold_in(key_list[7], part), 71), part)
    values = scatter_about(own_keys[2], (TOKENS, MODEL_WIDTH), 1.0, 6.0, ((0, 32),))
    value_layer_input = scatter_about(own_keys[3], (TOKENS, MODEL_WIDTH), 1.0, 6.0, ((0, 32),))
    adapter_down_weight = scatter_about(key_list[4], (MODEL_WIDTH, ADAPTER_RANK), MODEL_WIDTH ** -0.5, 0.09375)
    adapter_up_weight = scatter_about(key_list[5], (MODEL_WIDTH, ADAPTER_RANK), ADAPTER_RANK ** -0.5, 0.75)
    neighbors = draw_neighbors(jax.random.fold_in(jax.random.fold_in(key_list[7], part), 71), part)
    return dict(queries=queries, keys=keys, values=values, value_layer_input=value_layer_input, adapter_down_weight=adapter_down_weight, adapter_up_weight=adapter_up_weight, neighbors=neighbors)


def full_heads(queries, keys, values):
    total = queries.shape[0]
    block = min(512, total)
    scale = HD ** -0.5
    keys_float = keys.astype(jnp.float32)
    values_float = values.astype(jnp.float32)

    def one_block(query_block):
        scores = jnp.einsum("qhd,khd->hqk", query_block.astype(jnp.float32), keys_float) * scale
        top = jnp.max(scores, axis=2, keepdims=True)
        expo = jnp.exp(scores - top)
        weights = (expo / jnp.sum(expo, axis=2, keepdims=True)).astype(jnp.bfloat16)
        return jnp.einsum("hqk,khd->qhd", weights.astype(jnp.float32), values_float).astype(jnp.bfloat16)

    blocks = queries.reshape(total // block, block, queries.shape[1], queries.shape[2])
    return lax.map(one_block, blocks).reshape(queries.shape)


def contract_rows(left, right):
    return lax.dot_general(left.astype(jnp.float32), right.astype(jnp.float32), (((0,), (0,)), ((), ())), precision=lax.Precision.HIGHEST, preferred_element_type=jnp.float32)


def reference(queries, keys, values, value_layer_input, adapter_down_weight, adapter_up_weight, neighbors):
    teacher = full_heads(queries.reshape(TOKENS, H, HD), keys.reshape(TOKENS, H, HD), values.reshape(TOKENS, H, HD)).reshape(TOKENS, MODEL_WIDTH)
    adapter_down_rows = jnp.dot(value_layer_input, adapter_down_weight, preferred_element_type=jnp.float32).astype(jnp.bfloat16)
    adapter_value_term = lax.dot_general(adapter_down_rows, adapter_up_weight, (((1,), (1,)), ((), ())), preferred_element_type=jnp.float32)
    learner_values = (values.astype(jnp.float32) + adapter_value_term).astype(jnp.bfloat16)
    up_float = adapter_up_weight.astype(jnp.float32)
    border_width = ((TOK_DEV, TOK_DEV), (0, 0))
    keys_pad = jnp.pad(keys, border_width)
    values_pad = jnp.pad(learner_values, border_width)
    input_pad = jnp.pad(value_layer_input, border_width)
    padded_down_rows = jnp.pad(adapter_down_rows, border_width)
    slots = jnp.arange(3 * TPD, dtype=jnp.int32)
    scale = HD ** -0.5
    factor = TOKENS ** -0.5

    def slab_step(carry, slab):
        start = (slab * TOK_DEV).astype(jnp.int32)
        win_keys = lax.dynamic_slice_in_dim(keys_pad, start, 3 * TOK_DEV, 0).reshape(3 * TOK_DEV, H, HD)
        win_values = lax.dynamic_slice_in_dim(values_pad, start, 3 * TOK_DEV, 0).reshape(3 * TOK_DEV, H, HD)
        win_input = lax.dynamic_slice_in_dim(input_pad, start, 3 * TOK_DEV, 0)
        win_down = lax.dynamic_slice_in_dim(padded_down_rows, start, 3 * TOK_DEV, 0)
        slab_queries = lax.dynamic_slice_in_dim(queries, start, TOK_DEV, 0).reshape(TOK_DEV, H, HD)
        slab_teacher = lax.dynamic_slice_in_dim(teacher, start, TOK_DEV, 0)
        slab_tiles = lax.dynamic_slice_in_dim(neighbors, (slab * TPD).astype(jnp.int32), TPD, 0)
        offsets = slab_tiles - (slab - 1) * TPD
        tile_mask = jnp.any(offsets[:, :, None] == slots[None, None, :], axis=1)
        token_mask = jnp.broadcast_to(tile_mask[:, None, :, None], (TPD, TILE, 3 * TPD, TILE)).reshape(TOK_DEV, 3 * TOK_DEV)
        scores = jnp.einsum("qhd,khd->hqk", slab_queries.astype(jnp.float32), win_keys.astype(jnp.float32)) * scale
        scores = jnp.where(token_mask[None], scores, -1e30)
        top = jnp.max(scores, axis=2, keepdims=True)
        expo = jnp.exp(scores - top)
        weights = (expo / jnp.sum(expo, axis=2, keepdims=True)).astype(jnp.bfloat16)
        student = jnp.einsum("hqk,khd->qhd", weights.astype(jnp.float32), win_values.astype(jnp.float32)).reshape(TOK_DEV, MODEL_WIDTH)
        output_grad = ((student - slab_teacher.astype(jnp.float32)) * factor).astype(jnp.bfloat16)
        key_gradient = jnp.einsum("hqk,qhd->khd", weights.astype(jnp.float32), output_grad.reshape(TOK_DEV, H, HD).astype(jnp.float32))
        key_gradient = key_gradient.reshape(3 * TOK_DEV, MODEL_WIDTH)
        adapter_latent_rows = jnp.dot(key_gradient, up_float, precision=lax.Precision.HIGHEST, preferred_element_type=jnp.float32)
        grad_down = carry[0] + contract_rows(win_input, adapter_latent_rows)
        grad_up = carry[1] + contract_rows(key_gradient, win_down)
        return (grad_down, grad_up), student.astype(jnp.bfloat16)

    zeros = jnp.zeros((MODEL_WIDTH, ADAPTER_RANK), jnp.float32)
    (grad_down, grad_up), outputs = lax.scan(slab_step, (zeros, zeros), jnp.arange(N_CONTEXT, dtype=jnp.int32))
    return outputs.reshape(TOKENS, MODEL_WIDTH), grad_down, grad_up
```

```python
import functools
import math

import jax
import jax.numpy as jnp
from jax import lax
from jax.experimental import pallas as pl
from jax.experimental.pallas import tpu as pltpu
from jax.sharding import PartitionSpec as P

MESH = pl.DeviceIdType.MESH
F32 = jnp.float32
BF16 = jnp.bfloat16

N = 32
NZ = 8
TOK = 128
HD = 128
RANK = 64
TILE = 64
TOKENS = N * TOK
WIDTH = N * HD
PAD = TOK
DROWS = 80
BQ = 2 * TOK
CK = 512
CV = 1024
EXP2_SCALE = math.log2(math.e) / math.sqrt(HD)


def ring_step(j):
    half = (j + 1) // 2
    return lax.rem(half * lax.rem(j, 2) + (NZ - half) * (1 - lax.rem(j, 2)), NZ)


def dot(a, b):
    return jnp.dot(a, b, preferred_element_type=F32)


def dot_tt(a, b, dims):
    return lax.dot_general(a, b, (dims, ((), ())), preferred_element_type=F32)


def kernel(
    q_hbm,
    k_hbm,
    v_hbm,
    x_hbm,
    down_hbm,
    up_hbm,
    nb_ref,
    out_hbm,
    gdown_ref,
    gup_ref,
    xbuf,
    dwbuf,
    upbuf,
    kbuf,
    vbuf,
    qbuf,
    keys_t,
    v_aug,
    svd,
    expand,
    scores,
    obuf,
    dbuf,
    hid,
    gup_t,
    gdn,
    rs_s1,
    rs_r1,
    rs_s2,
    rs_r2,
    load_sem,
    ssem,
    ksem,
    vsem,
    qsem,
    osem,
    dsem_s,
    dsem_a,
    dsem_b,
    rs_sem,
):
    me = lax.axis_index("context")
    y, z, c = me // 16, lax.rem(me // 2, NZ), lax.rem(me, 2)
    chip = me // 2
    lane = y * 2 + c

    def device(yy, zz, cc):
        return (yy * NZ + zz) * 2 + cc

    def remote(src, dst, send, recv, target):
        return pltpu.make_async_remote_copy(
            src_ref=src,
            dst_ref=dst,
            send_sem=send,
            recv_sem=recv,
            device_id={"context": target},
            device_id_type=MESH,
        )

    def cols(index):
        return pl.ds(pl.multiple_of(index * HD, HD), HD)

    def rows(index, count=TOK):
        return pl.ds(pl.multiple_of(index * TOK, TOK), count)

    def drain(ref, sem):
        pltpu.make_async_copy(ref, ref, sem).wait()

    load_x = pltpu.make_async_copy(x_hbm, xbuf, load_sem.at[0])
    load_dw = pltpu.make_async_copy(down_hbm, dwbuf, load_sem.at[1])
    load_up = pltpu.make_async_copy(up_hbm.at[rows(me)], upbuf, load_sem.at[2])
    load_x.start()
    load_dw.start()
    load_up.start()

    barrier = pltpu.get_barrier_semaphore()

    @pl.loop(1, N)
    def _(j):
        pl.semaphore_signal(
            barrier, inc=1, device_id={"context": lax.rem(me + j, N)}, device_id_type=MESH
        )

    for hbm, buf, sems in ((k_hbm, kbuf, ksem), (v_hbm, vbuf, vsem), (q_hbm, qbuf, qsem)):
        pltpu.make_async_copy(hbm.at[:, cols(me)], buf.at[rows(me)], sems.at[me]).start()

    keys_t[:, :PAD] = jnp.zeros((HD, PAD), BF16)
    keys_t[:, PAD + TOKENS :] = jnp.zeros((HD, PAD), BF16)
    svd[:PAD, :] = jnp.zeros((PAD, 2 * HD), BF16)
    svd[PAD + TOKENS :, :] = jnp.zeros((PAD, 2 * HD), BF16)
    hid[...] = jnp.zeros_like(hid)
    gup_t[...] = jnp.zeros_like(gup_t)
    slot_row = lax.broadcasted_iota(jnp.int32, (TOK, 3 * TOK), 0)
    slot_col = lax.broadcasted_iota(jnp.int32, (TOK, 3 * TOK), 1)
    expand[...] = jnp.where(slot_row - RANK == slot_col // TILE, 1.0, 0.0).astype(BF16)

    @pl.loop(0, N)
    def _(s):
        v_aug[rows(s), HD:] = jnp.ones((TOK, HD), BF16)

    load_x.wait()
    load_dw.wait()
    load_up.wait()
    down = dot(xbuf[...], dwbuf[...])
    mask_row = lax.broadcasted_iota(jnp.int32, (DROWS - RANK, TOK), 0)
    mask_col = lax.broadcasted_iota(jnp.int32, (DROWS - RANK, TOK), 1)
    mask = jnp.zeros((DROWS - RANK, TOK), F32)
    for slot in range(6):
        wanted = (me - 1) * 2 + slot
        seen = []
        for t in range(2):
            hit = jnp.float32(0.0)
            for e in range(4):
                hit = jnp.where(nb_ref[t, e] == wanted, jnp.float32(1.0), hit)
            seen.append(hit)
        mask = jnp.where(
            mask_row == slot, jnp.where(mask_col < TILE, seen[0], seen[1]), mask
        )
    dbuf[lane, z, :RANK, :] = down.T.astype(BF16)
    dbuf[lane, z, RANK:, :] = mask.astype(BF16)
    up = upbuf[...]

    pl.semaphore_wait(barrier, N - 1)

    @pl.loop(1, NZ)
    def _(j):
        remote(
            dbuf.at[lane, z],
            dbuf.at[lane, z],
            dsem_s.at[0],
            dsem_a,
            device(y, lax.rem(z + ring_step(j), NZ), c),
        ).start()

    def send_all(hbm, buf, send, sems):
        @pl.loop(1, N)
        def _(i):
            target = device(
                lax.rem(y + lax.rem(i // 2, 2), 2),
                lax.rem(z + ring_step(i // 4), NZ),
                lax.rem(c + lax.rem(i, 2), 2),
            )
            remote(hbm.at[:, cols(target)], buf.at[rows(me)], send, sems.at[me], target).start()

    send_all(k_hbm, kbuf, ssem.at[0], ksem)

    drain(dbuf.at[0, pl.ds(0, NZ - 1)], dsem_a)
    for dy, dc in ((0, 1), (1, 0), (1, 1)):
        remote(
            dbuf.at[lane],
            dbuf.at[lane],
            dsem_s.at[1],
            dsem_b.at[lane],
            device(lax.rem(y + dy, 2), z, lax.rem(c + dc, 2)),
        ).start()

    send_all(v_hbm, vbuf, ssem.at[1], vsem)
    send_all(q_hbm, qbuf, ssem.at[2], qsem)

    def source(i):
        return device(
            lax.rem(y + lax.rem(i // 2, 2), 2),
            lax.rem(z + NZ - ring_step(i // 4), NZ),
            lax.rem(c + lax.rem(i, 2), 2),
        )

    @pl.loop(0, N)
    def _(i):
        s = source(i)
        drain(kbuf.at[rows(s)], ksem.at[s])
        keys_t[:, rows(s + 1)] = kbuf[rows(s), :].T

    for dy, dc in ((0, 1), (1, 0), (1, 1)):
        other = lax.rem(y + dy, 2) * 2 + lax.rem(c + dc, 2)
        drain(dbuf.at[other], dsem_b.at[other])

    @pl.loop(0, N)
    def _(i):
        s = source(i)
        block = dbuf[
            (s // 16) * 2 + lax.rem(s, 2), lax.rem(s // 2, NZ)
        ]
        block = jnp.concatenate([block, jnp.zeros((TOK - DROWS, TOK), BF16)], axis=0).T
        drain(vbuf.at[rows(s)], vsem.at[s])
        value = vbuf[rows(s), :]
        v_aug[rows(s), :HD] = value
        term = dot_tt(block[:, :RANK], up, ((1,), (1,)))
        svd[rows(s + 1), :HD] = (value.astype(F32) + term).astype(BF16)
        svd[rows(s + 1), HD:] = block

    up_t = up.T

    @pl.loop(0, N // 2)
    def _(i):
        pair = lax.rem(y + lax.rem(i, 2), 2) * NZ + lax.rem(z + NZ - ring_step(i // 2), NZ)
        for u in range(2):
            drain(qbuf.at[rows(2 * pair + u)], qsem.at[2 * pair + u])
        query = qbuf[rows(2 * pair, BQ), :]
        top = None
        for n in range(TOKENS // CK):
            chunk = dot(query, keys_t[:, PAD + n * CK : PAD + (n + 1) * CK])
            scores[:, n * CK : (n + 1) * CK] = chunk
            for m in range(CK // HD):
                part = chunk[:, m * HD : (m + 1) * HD]
                top = part if top is None else jnp.maximum(top, part)
        top = jnp.max(top, axis=1, keepdims=True)
        total = None
        for n in range(TOKENS // CV):
            expo = jnp.exp2((scores[:, n * CV : (n + 1) * CV] - top) * EXP2_SCALE)
            part = dot(expo.astype(BF16), v_aug[n * CV : (n + 1) * CV, :])
            total = part if total is None else total + part
        teacher = (total[:, :HD] / total[:, HD:]).astype(BF16).astype(F32)
        for u in range(2):
            s = 2 * pair + u
            window = rows(s, 3 * TOK)
            raw = dot(qbuf[rows(s), :], keys_t[:, window])
            seen = dot(svd[rows(s + 1), HD:], expand[...])
            raw = jnp.where(seen > 0.5, raw, -1e30)
            high = jnp.max(raw, axis=1, keepdims=True)
            expo = jnp.exp2((raw - high) * EXP2_SCALE)
            weights = (expo / jnp.sum(expo, axis=1, keepdims=True)).astype(BF16)
            mixed = dot(weights, svd[window, :])
            student = mixed[:, :HD]
            obuf[rows(s), :] = student.astype(BF16)
            grad = ((student - teacher[u * TOK : (u + 1) * TOK, :]) * (TOKENS**-0.5)).astype(BF16)
            latent = dot_tt(up_t, grad, ((1,), (1,))).astype(BF16)
            hid[:, window] += dot(latent, weights)
            gup_t[...] += dot_tt(mixed[:, HD : HD + RANK].astype(BF16), grad, ((0,), (0,)))
        for u in range(2):
            s = 2 * pair + u

            @pl.when(s == me)
            def _():
                pltpu.make_async_copy(
                    obuf.at[rows(s)], out_hbm.at[:, cols(me)], osem.at[2]
                ).start()

            @pl.when(s != me)
            def _():
                remote(
                    obuf.at[rows(s)], out_hbm.at[:, cols(me)], osem.at[0], osem.at[1], s
                ).start()

    gup_ref[...] = gup_t[...].T

    def reduce_scatter(src, offset, k):
        def block(owner_chip, owner_core):
            return src[:, pl.ds(pl.multiple_of(offset + (2 * owner_chip + owner_core) * TOK, TOK), TOK)]

        @pl.loop(0, N // 2)
        def _(m):
            rs_s1[k, m] = block(m, 1 - c).astype(BF16)

        copy = remote(rs_s1.at[k], rs_r1.at[k], rs_sem.at[k, 0], rs_sem.at[k, 1], 2 * chip + 1 - c)
        copy.start()
        copy.wait()

        @pl.loop(0, N // 2)
        def _(m):
            rs_s2[k, m] = (block(m, c) + rs_r1[k, m].astype(F32)).astype(BF16)

        @pl.loop(1, N // 2)
        def _(i):
            owner = lax.rem(y + lax.rem(i, 2), 2) * NZ + lax.rem(z + ring_step(i // 2), NZ)
            remote(
                rs_s2.at[k, owner], rs_r2.at[k, chip], rs_sem.at[k, 2], rs_sem.at[k, 3], 2 * owner + c
            ).start()

        rs_r2[k, chip] = rs_s2[k, chip]
        drain(rs_r2.at[k, pl.ds(0, N // 2 - 1)], rs_sem.at[k, 3])
        result = rs_r2[k, 0].astype(F32)
        for m in range(1, N // 2):
            result = result + rs_r2[k, m].astype(F32)
        return result

    hidden = reduce_scatter(hid, PAD, 0)
    hidden_hi = hidden.astype(BF16)
    hidden_lo = (hidden - hidden_hi.astype(F32)).astype(BF16)
    gdn[...] = dot(hidden_hi, xbuf[...]) + dot(hidden_lo, xbuf[...])
    gdown_ref[...] = reduce_scatter(gdn, 0, 1).T

    for a in range(3):
        drain(kbuf.at[pl.ds(0, (N - 1) * TOK)], ssem.at[a])
    drain(dbuf.at[0, pl.ds(0, NZ - 1)], dsem_s.at[0])
    drain(dbuf.at[pl.ds(0, 3)], dsem_s.at[1])
    for k in range(2):
        drain(rs_s2.at[k, pl.ds(0, N // 2 - 1)], rs_sem.at[k, 2])
    drain(obuf.at[pl.ds(0, (N - 1) * TOK)], osem.at[0])
    drain(obuf.at[pl.ds(0, (N - 1) * TOK)], osem.at[1])
    drain(obuf.at[pl.ds(0, TOK)], osem.at[2])


def local(
    queries, keys, values, value_layer_input, adapter_down_weight, adapter_up_weight, neighbors
):
    anywhere = pl.BlockSpec(memory_space=pl.ANY)
    vmem = pl.BlockSpec(memory_space=pltpu.VMEM)
    dma = pltpu.SemaphoreType.DMA
    return pl.pallas_call(
        kernel,
        out_shape=(
            jax.ShapeDtypeStruct((TOK, WIDTH), BF16),
            jax.ShapeDtypeStruct((TOK, RANK), F32),
            jax.ShapeDtypeStruct((TOK, RANK), F32),
        ),
        in_specs=[anywhere] * 6 + [pl.BlockSpec(memory_space=pltpu.SMEM)],
        out_specs=(anywhere, vmem, vmem),
        scratch_shapes=[
            pltpu.VMEM((TOK, WIDTH), BF16),
            pltpu.VMEM((WIDTH, RANK), BF16),
            pltpu.VMEM((HD, RANK), BF16),
            pltpu.VMEM((TOKENS, HD), BF16),
            pltpu.VMEM((TOKENS, HD), BF16),
            pltpu.VMEM((TOKENS, HD), BF16),
            pltpu.VMEM((HD, TOKENS + 2 * PAD), BF16),
            pltpu.VMEM((TOKENS, 2 * HD), BF16),
            pltpu.VMEM((TOKENS + 2 * PAD, 2 * HD), BF16),
            pltpu.VMEM((TOK, 3 * TOK), BF16),
            pltpu.VMEM((BQ, TOKENS), F32),
            pltpu.VMEM((TOKENS, HD), BF16),
            pltpu.VMEM((4, NZ, DROWS, TOK), BF16),
            pltpu.VMEM((RANK, TOKENS + 2 * PAD), F32),
            pltpu.VMEM((RANK, HD), F32),
            pltpu.VMEM((RANK, WIDTH), F32),
            pltpu.VMEM((2, N // 2, RANK, TOK), BF16),
            pltpu.VMEM((2, N // 2, RANK, TOK), BF16),
            pltpu.VMEM((2, N // 2, RANK, TOK), BF16),
            pltpu.VMEM((2, N // 2, RANK, TOK), BF16),
            dma((3,)),
            dma((3,)),
            dma((N,)),
            dma((N,)),
            dma((N,)),
            dma((3,)),
            dma((2,)),
            dma,
            dma((4,)),
            dma((2, 4)),
        ],
        compiler_params=pltpu.CompilerParams(
            collective_id=0, has_side_effects=True, vmem_limit_bytes=60 << 20
        ),
    )(queries, keys, values, value_layer_input, adapter_down_weight, adapter_up_weight, neighbors)


def solution(mesh):
    rows_split = P(("video", "context"), None)
    return jax.shard_map(
        local,
        mesh=mesh,
        in_specs=(rows_split,) * 4 + (P(), P(), rows_split),
        out_specs=(rows_split,) * 3,
        check_vma=False,
    )
```

```python
import math

import jax
import jax.numpy as jnp
from jax import lax
from jax.experimental import pallas as pl
from jax.experimental.pallas import tpu as pltpu
from jax.sharding import PartitionSpec as P

MESH = pl.DeviceIdType.MESH
F32 = jnp.float32
BF16 = jnp.bfloat16

N = 32
NZ = 8
TOK = 128
HD = 128
RANK = 64
TILE = 64
TOKENS = N * TOK
WIDTH = N * HD
PAD = TOK
DROWS = 80
BQ = 4 * TOK
CK = 4 * TOK
EXP2_SCALE = math.log2(math.e) / math.sqrt(HD)


def ring_step(j):
    half = (j + 1) // 2
    return lax.rem(half * lax.rem(j, 2) + (NZ - half) * (1 - lax.rem(j, 2)), NZ)


def dot(a, b):
    return jnp.dot(a, b, preferred_element_type=F32)


def dot_tt(a, b, dims):
    return lax.dot_general(a, b, (dims, ((), ())), preferred_element_type=F32)


def kernel(
    q_hbm,
    k_hbm,
    v_hbm,
    x_hbm,
    down_hbm,
    up_hbm,
    nb_ref,
    out_hbm,
    gdown_ref,
    gup_ref,
    xbuf,
    dwbuf,
    up_t,
    kbuf,
    vbuf,
    qbuf,
    keys_t,
    v_aug,
    svd,
    expand,
    scores0,
    scores1,
    tops0,
    tops1,
    high,
    acc,
    wts,
    stu,
    mixd,
    obuf,
    dbuf,
    hid,
    gdn,
    hid_hi,
    hid_lo,
    rs_s1,
    rs_r1,
    rs_s2,
    rs_r2,
    load_sem,
    ssem,
    ksem,
    vsem,
    qsem,
    osem,
    dsem_s,
    dsem_a,
    dsem_b,
    rs_sem,
    rs_pair,
):
    me = lax.axis_index("context")
    y, z, c = me // 16, lax.rem(me // 2, NZ), lax.rem(me, 2)
    chip = me // 2
    lane = y * 2 + c

    def device(yy, zz, cc):
        return (yy * NZ + zz) * 2 + cc

    def remote(src, dst, send, recv, target):
        return pltpu.make_async_remote_copy(
            src_ref=src,
            dst_ref=dst,
            send_sem=send,
            recv_sem=recv,
            device_id={"context": target},
            device_id_type=MESH,
        )

    def cols(index):
        return pl.ds(pl.multiple_of(index * HD, HD), HD)

    def rows(index, count=TOK):
        return pl.ds(pl.multiple_of(index * TOK, TOK), count)

    def drain(ref, sem):
        pltpu.make_async_copy(ref, ref, sem).wait()

    load_x = pltpu.make_async_copy(x_hbm, xbuf, load_sem.at[0])
    load_dw = pltpu.make_async_copy(down_hbm, dwbuf, load_sem.at[1])
    load_up = pltpu.make_async_copy(up_hbm.at[:, cols(me)], up_t, load_sem.at[2])
    load_x.start()
    load_dw.start()
    load_up.start()

    barrier = pltpu.get_barrier_semaphore()

    @pl.loop(1, N)
    def _(j):
        pl.semaphore_signal(
            barrier, inc=1, device_id={"context": lax.rem(me + j, N)}, device_id_type=MESH
        )

    for hbm, buf, sems in ((k_hbm, kbuf, ksem), (v_hbm, vbuf, vsem), (q_hbm, qbuf, qsem)):
        pltpu.make_async_copy(hbm.at[:, cols(me)], buf.at[rows(me)], sems.at[me]).start()

    keys_t[:, :PAD] = jnp.zeros((HD, PAD), BF16)
    keys_t[:, PAD + TOKENS :] = jnp.zeros((HD, PAD), BF16)
    svd[:PAD, :] = jnp.zeros((PAD, 2 * HD), BF16)
    svd[PAD + TOKENS :, :] = jnp.zeros((PAD, 2 * HD), BF16)
    hid[...] = jnp.zeros_like(hid)
    gup_ref[...] = jnp.zeros_like(gup_ref)
    slot_row = lax.broadcasted_iota(jnp.int32, (TOK, 3 * TOK), 0)
    slot_col = lax.broadcasted_iota(jnp.int32, (TOK, 3 * TOK), 1)
    expand[...] = jnp.where(slot_row - RANK == slot_col // TILE, 1.0, 0.0).astype(BF16)

    @pl.loop(0, N)
    def _(s):
        v_aug[rows(s), HD:] = jnp.ones((TOK, HD), BF16)
        high[rows(s), :] = jnp.full((TOK, HD), -1e30, F32)
        acc[rows(s), :] = jnp.zeros((TOK, 2 * HD), F32)

    load_x.wait()
    load_dw.wait()
    load_up.wait()
    mask_row = lax.broadcasted_iota(jnp.int32, (DROWS - RANK, TOK), 0)
    mask_col = lax.broadcasted_iota(jnp.int32, (DROWS - RANK, TOK), 1)
    mask = jnp.zeros((DROWS - RANK, TOK), F32)
    for slot in range(6):
        wanted = (me - 1) * 2 + slot
        seen = []
        for t in range(2):
            hit = jnp.float32(0.0)
            for e in range(4):
                hit = jnp.where(nb_ref[t, e] == wanted, jnp.float32(1.0), hit)
            seen.append(hit)
        mask = jnp.where(
            mask_row == slot, jnp.where(mask_col < TILE, seen[0], seen[1]), mask
        )
    dbuf[lane, z, :RANK, :] = dot_tt(dwbuf[...], xbuf[...], ((1,), (1,))).astype(BF16)
    dbuf[lane, z, RANK:, :] = mask.astype(BF16)

    pl.semaphore_wait(barrier, N - 1)

    @pl.loop(1, NZ)
    def _(j):
        remote(
            dbuf.at[lane, z],
            dbuf.at[lane, z],
            dsem_s.at[0],
            dsem_a,
            device(y, lax.rem(z + ring_step(j), NZ), c),
        ).start()

    def send_all(*arrays):
        @pl.loop(1, N)
        def _(i):
            target = device(
                lax.rem(y + lax.rem(i // 2, 2), 2),
                lax.rem(z + ring_step(i // 4), NZ),
                lax.rem(c + lax.rem(i, 2), 2),
            )
            for hbm, buf, send, sems in arrays:
                remote(
                    hbm.at[:, cols(target)], buf.at[rows(me)], send, sems.at[me], target
                ).start()

    send_all((q_hbm, qbuf, ssem.at[0], qsem))

    drain(dbuf.at[0, pl.ds(0, NZ - 1)], dsem_a)
    for dy, dc in ((0, 1), (1, 0), (1, 1)):
        remote(
            dbuf.at[lane],
            dbuf.at[lane],
            dsem_s.at[1],
            dsem_b.at[lane],
            device(lax.rem(y + dy, 2), z, lax.rem(c + dc, 2)),
        ).start()

    send_all((k_hbm, kbuf, ssem.at[1], ksem), (v_hbm, vbuf, ssem.at[2], vsem))

    for dy, dc in ((0, 1), (1, 0), (1, 1)):
        other = lax.rem(y + dy, 2) * 2 + lax.rem(c + dc, 2)
        drain(dbuf.at[other], dsem_b.at[other])

    @pl.loop(0, N)
    def _(s):
        drain(qbuf.at[rows(s)], qsem.at[s])

    def position(j):
        return lax.rem(z + NZ - ring_step(j), NZ)

    def send_out(j):
        s = device(lax.rem(j // 2, 2), position(j // 4), lax.rem(j, 2))

        @pl.when(s == me)
        def _():
            pltpu.make_async_copy(obuf.at[rows(s)], out_hbm.at[:, cols(me)], osem.at[2]).start()

        @pl.when(s != me)
        def _():
            remote(
                obuf.at[rows(s)], out_hbm.at[:, cols(me)], osem.at[0], osem.at[1], s
            ).start()

    def done(k):
        f = (k + 1) // 2
        return (2 * f - 3) * ((f + 2) // 4) + 3 * (k // NZ)

    @pl.loop(0, NZ)
    def _(g):
        place = position(g)
        for yy in range(2):
            for cc in range(2):
                s = device(yy, place, cc)
                drain(kbuf.at[rows(s)], ksem.at[s])
                keys_t[:, rows(s + 1)] = kbuf[rows(s), :].T
                block = jnp.concatenate(
                    [dbuf[yy * 2 + cc, place], jnp.zeros((TOK - DROWS, TOK), BF16)], axis=0
                ).T
                term = dot(block[:, :RANK], up_t[...])
                drain(vbuf.at[rows(s)], vsem.at[s])
                value = vbuf[rows(s), :]
                v_aug[rows(s), :HD] = value
                svd[rows(s + 1), :HD] = (value.astype(F32) + term).astype(BF16)
                svd[rows(s + 1), HD:] = block

        @pl.loop(done(g), done(g + 1))
        def _(j):
            for lane_at in range(4):
                s = device(lane_at // 2, position(j), lane_at % 2)
                window = rows(s, 3 * TOK)
                raw = dot(qbuf[rows(s), :], keys_t[:, window])
                seen = dot(svd[rows(s + 1), HD:], expand[...])
                raw = jnp.where(seen > 0.5, raw, -1e30)
                most = jnp.max(raw, axis=1, keepdims=True)
                expo = jnp.exp2((raw - most) * EXP2_SCALE)
                weights = (expo / jnp.sum(expo, axis=1, keepdims=True)).astype(BF16)
                mixed = dot(weights, svd[window, :])
                wts[s] = weights
                stu[rows(s), :] = mixed[:, :HD]
                obuf[rows(s), :] = mixed[:, :HD].astype(BF16)
                mixd[rows(s), :] = mixed[:, HD:].astype(BF16)

        @pl.loop(4 * done(g), 4 * done(g + 1))
        def _(j):
            send_out(j)

        firsts = [(yy * NZ + place) * 2 for yy in range(2)]

        def score(i, scores, tops):
            block = pl.ds(pl.multiple_of(i * BQ, BQ), BQ)
            query = qbuf[block, :]
            top = high[block, :]
            for yy, first in enumerate(firsts):
                chunk = dot(query, keys_t[:, rows(first + 1, 2 * TOK)])
                scores[:, yy * 2 * TOK : (yy + 1) * 2 * TOK] = chunk
                top = jnp.maximum(top, jnp.maximum(chunk[:, :HD], chunk[:, HD:]))
            tops[...] = jnp.broadcast_to(jnp.max(top, axis=1, keepdims=True), (BQ, HD))

        def update(i, scores, tops):
            block = pl.ds(pl.multiple_of(i * BQ, BQ), BQ)
            new = tops[...]
            alpha = jnp.exp2((high[block, :] - new) * EXP2_SCALE)
            high[block, :] = new
            part = None
            for yy, first in enumerate(firsts):
                expo = jnp.concatenate(
                    [
                        jnp.exp2(
                            (scores[:, (2 * yy + h) * HD : (2 * yy + h + 1) * HD] - new)
                            * EXP2_SCALE
                        ).astype(BF16)
                        for h in range(2)
                    ],
                    axis=1,
                )
                term = dot(expo, v_aug[rows(first, 2 * TOK), :])
                part = term if part is None else part + term
            acc[block, :HD] = acc[block, :HD] * alpha + part[:, :HD]
            acc[block, HD:] = acc[block, HD:] * alpha + part[:, HD:]

        blocks = TOKENS // BQ
        score(0, scores0, tops0)

        @pl.loop(0, blocks // 2)
        def _(i):
            update(2 * i, scores0, tops0)
            score(2 * i + 1, scores1, tops1)
            update(2 * i + 1, scores1, tops1)
            score(lax.rem(2 * i + 2, blocks), scores0, tops0)

    def block(src, offset, owner):
        return src[:, pl.ds(pl.multiple_of(offset + owner * TOK, TOK), TOK)]

    def exchange(k, src, offset, ch):
        for m in range(4):
            owner = 4 * ch + m
            rs_s1[k, owner] = block(src, offset, 2 * owner + 1 - c).astype(BF16)
        part = pl.ds(4 * ch, 4)
        remote(
            rs_s1.at[k, part], rs_r1.at[k, part], rs_sem.at[k, 0], rs_pair.at[k, ch], me + 1 - 2 * c
        ).start()

    def scatter(k, src, offset):
        @pl.loop(0, 4)
        def _(ch):
            drain(rs_r1.at[k, pl.ds(4 * ch, 4)], rs_pair.at[k, ch])
            for m in range(4):
                owner = 4 * ch + m
                rs_s2[k, owner] = (
                    block(src, offset, 2 * owner + c) + rs_r1[k, owner].astype(F32)
                ).astype(BF16)

        @pl.loop(1, N // 2)
        def _(i):
            owner = lax.rem(y + lax.rem(i, 2), 2) * NZ + lax.rem(z + ring_step(i // 2), NZ)
            remote(
                rs_s2.at[k, owner], rs_r2.at[k, chip], rs_sem.at[k, 1], rs_sem.at[k, 2], 2 * owner + c
            ).start()

        rs_r2[k, chip] = rs_s2[k, chip]

    def total(k):
        drain(rs_r2.at[k, pl.ds(0, N // 2 - 1)], rs_sem.at[k, 2])
        result = rs_r2[k, 0].astype(F32)
        for m in range(1, N // 2):
            result = result + rs_r2[k, m].astype(F32)
        return result

    @pl.loop(0, 4)
    def _(ch):
        def adapter(s):
            teacher = (acc[rows(s), :HD] / acc[rows(s), HD:]).astype(BF16).astype(F32)
            grad = ((stu[rows(s), :] - teacher) * (TOKENS**-0.5)).astype(BF16)
            latent = dot_tt(up_t[...], grad, ((1,), (1,))).astype(BF16)
            return (
                dot(latent, wts[s]),
                dot_tt(mixd[rows(s), :RANK], grad, ((0,), (0,))),
            )

        @pl.loop(0, 2)
        def _(h):
            slabs = [8 * ch + 4 * h + u for u in range(4)]
            terms = [adapter(s) for s in slabs]
            for s, term in zip(slabs, terms):
                hid[:, rows(s, 3 * TOK)] += term[0]
            gup_ref[...] += (terms[0][1] + terms[1][1]) + (terms[2][1] + terms[3][1])

        @pl.when(ch > 0)
        def _():
            exchange(0, hid, PAD, ch - 1)

    exchange(0, hid, PAD, 3)


    scatter(0, hid, PAD)

    hidden = total(0)
    hid_hi[...] = hidden.astype(BF16)
    hid_lo[...] = (hidden - hidden.astype(BF16).astype(F32)).astype(BF16)

    @pl.loop(0, 4)
    def _(ch):
        part = pl.ds(pl.multiple_of(ch * 8 * TOK, TOK), 8 * TOK)
        gdn[:, part] = dot(hid_hi[...], xbuf[:, part]) + dot(hid_lo[...], xbuf[:, part])
        exchange(1, gdn, 0, ch)

    scatter(1, gdn, 0)
    gdown_ref[...] = total(1)

    for a in range(3):
        drain(kbuf.at[pl.ds(0, (N - 1) * TOK)], ssem.at[a])
    drain(dbuf.at[0, pl.ds(0, NZ - 1)], dsem_s.at[0])
    drain(dbuf.at[pl.ds(0, 3)], dsem_s.at[1])
    for k in range(2):
        drain(rs_s1.at[k], rs_sem.at[k, 0])
        drain(rs_s2.at[k, pl.ds(0, N // 2 - 1)], rs_sem.at[k, 1])
    drain(obuf.at[pl.ds(0, (N - 1) * TOK)], osem.at[0])
    drain(obuf.at[pl.ds(0, (N - 1) * TOK)], osem.at[1])
    drain(obuf.at[pl.ds(0, TOK)], osem.at[2])


def local(
    queries, keys, values, value_layer_input, adapter_down_weight, adapter_up_weight, neighbors
):
    anywhere = pl.BlockSpec(memory_space=pl.ANY)
    vmem = pl.BlockSpec(memory_space=pltpu.VMEM)
    dma = pltpu.SemaphoreType.DMA
    student_out, grad_down, grad_up = pl.pallas_call(
        kernel,
        out_shape=(
            jax.ShapeDtypeStruct((TOK, WIDTH), BF16),
            jax.ShapeDtypeStruct((RANK, HD), F32),
            jax.ShapeDtypeStruct((RANK, HD), F32),
        ),
        in_specs=[anywhere] * 6 + [pl.BlockSpec(memory_space=pltpu.SMEM)],
        out_specs=(anywhere, vmem, vmem),
        scratch_shapes=[
            pltpu.VMEM((TOK, WIDTH), BF16),
            pltpu.VMEM((RANK, WIDTH), BF16),
            pltpu.VMEM((RANK, HD), BF16),
            pltpu.VMEM((TOKENS, HD), BF16),
            pltpu.VMEM((TOKENS, HD), BF16),
            pltpu.VMEM((TOKENS, HD), BF16),
            pltpu.VMEM((HD, TOKENS + 2 * PAD), BF16),
            pltpu.VMEM((TOKENS, 2 * HD), BF16),
            pltpu.VMEM((TOKENS + 2 * PAD, 2 * HD), BF16),
            pltpu.VMEM((TOK, 3 * TOK), BF16),
            pltpu.VMEM((BQ, CK), F32),
            pltpu.VMEM((BQ, CK), F32),
            pltpu.VMEM((BQ, HD), F32),
            pltpu.VMEM((BQ, HD), F32),
            pltpu.VMEM((TOKENS, HD), F32),
            pltpu.VMEM((TOKENS, 2 * HD), F32),
            pltpu.VMEM((N, TOK, 3 * TOK), BF16),
            pltpu.VMEM((TOKENS, HD), F32),
            pltpu.VMEM((TOKENS, HD), BF16),
            pltpu.VMEM((TOKENS, HD), BF16),
            pltpu.VMEM((4, NZ, DROWS, TOK), BF16),
            pltpu.VMEM((RANK, TOKENS + 2 * PAD), F32),
            pltpu.VMEM((RANK, WIDTH), F32),
            pltpu.VMEM((RANK, TOK), BF16),
            pltpu.VMEM((RANK, TOK), BF16),
            pltpu.VMEM((2, N // 2, RANK, TOK), BF16),
            pltpu.VMEM((2, N // 2, RANK, TOK), BF16),
            pltpu.VMEM((2, N // 2, RANK, TOK), BF16),
            pltpu.VMEM((2, N // 2, RANK, TOK), BF16),
            dma((3,)),
            dma((3,)),
            dma((N,)),
            dma((N,)),
            dma((N,)),
            dma((3,)),
            dma((2,)),
            dma,
            dma((4,)),
            dma((2, 3)),
            dma((2, 4)),
        ],
        compiler_params=pltpu.CompilerParams(
            collective_id=0, has_side_effects=True, vmem_limit_bytes=60 << 20
        ),
    )(
        queries,
        keys,
        values,
        value_layer_input,
        adapter_down_weight.T,
        adapter_up_weight.T,
        neighbors,
    )
    return student_out, grad_down.T, grad_up.T


def solution(mesh):
    rows_split = P(("video", "context"), None)
    return jax.shard_map(
        local,
        mesh=mesh,
        in_specs=(rows_split,) * 4 + (P(), P(), rows_split),
        out_specs=(rows_split,) * 3,
        check_vma=False,
    )
```

```python
import math

import jax
import jax.numpy as jnp
from jax import lax
from jax.experimental import pallas as pl
from jax.experimental.pallas import tpu as pltpu
from jax.sharding import PartitionSpec as P

MESH = pl.DeviceIdType.MESH
F32 = jnp.float32
BF16 = jnp.bfloat16

N = 32
NZ = 8
TOK = 128
HD = 128
RANK = 64
TILE = 64
TOKENS = N * TOK
WIDTH = N * HD
PAD = TOK
DROWS = 80
BQ = 4 * TOK
CK = 4 * TOK
EXP2_SCALE = math.log2(math.e) / math.sqrt(HD)


def ring_step(j):
    half = (j + 1) // 2
    return lax.rem(half * lax.rem(j, 2) + (NZ - half) * (1 - lax.rem(j, 2)), NZ)


def dot(a, b):
    return jnp.dot(a, b, preferred_element_type=F32)


def dot_tt(a, b, dims):
    return lax.dot_general(a, b, (dims, ((), ())), preferred_element_type=F32)


def kernel(
    q_hbm,
    k_hbm,
    v_hbm,
    x_hbm,
    down_hbm,
    up_hbm,
    nb_ref,
    out_hbm,
    gdown_ref,
    gup_ref,
    xbuf,
    dwbuf,
    up_t,
    kbuf,
    vbuf,
    qbuf,
    keys_t,
    v_aug,
    svd,
    expand,
    scores0,
    scores1,
    tops0,
    tops1,
    high,
    acc,
    wts,
    stu,
    mixd,
    obuf,
    dbuf,
    hid,
    gdn,
    hid_hi,
    hid_lo,
    rs_s1,
    rs_r1,
    rs_s2,
    rs_r2,
    load_sem,
    ssem,
    ksem,
    vsem,
    qsem,
    osem,
    dsem_s,
    dsem_a,
    dsem_b,
    rs_sem,
    rs_pair,
):
    me = lax.axis_index("context")
    y, z, c = me // 16, lax.rem(me // 2, NZ), lax.rem(me, 2)
    chip = me // 2
    lane = y * 2 + c

    def device(yy, zz, cc):
        return (yy * NZ + zz) * 2 + cc

    def remote(src, dst, send, recv, target):
        return pltpu.make_async_remote_copy(
            src_ref=src,
            dst_ref=dst,
            send_sem=send,
            recv_sem=recv,
            device_id={"context": target},
            device_id_type=MESH,
        )

    def cols(index):
        return pl.ds(pl.multiple_of(index * HD, HD), HD)

    def rows(index, count=TOK):
        return pl.ds(pl.multiple_of(index * TOK, TOK), count)

    def drain(ref, sem):
        pltpu.make_async_copy(ref, ref, sem).wait()

    load_x = pltpu.make_async_copy(x_hbm, xbuf, load_sem.at[0])
    load_dw = pltpu.make_async_copy(down_hbm, dwbuf, load_sem.at[1])
    load_up = pltpu.make_async_copy(up_hbm.at[:, cols(me)], up_t, load_sem.at[2])
    load_x.start()
    load_dw.start()
    load_up.start()

    barrier = pltpu.get_barrier_semaphore()

    @pl.loop(1, N)
    def _(j):
        pl.semaphore_signal(
            barrier, inc=1, device_id={"context": lax.rem(me + j, N)}, device_id_type=MESH
        )

    for hbm, buf, sems in ((k_hbm, kbuf, ksem), (v_hbm, vbuf, vsem), (q_hbm, qbuf, qsem)):
        pltpu.make_async_copy(hbm.at[:, cols(me)], buf.at[rows(me)], sems.at[me]).start()

    keys_t[:, :PAD] = jnp.zeros((HD, PAD), BF16)
    keys_t[:, PAD + TOKENS :] = jnp.zeros((HD, PAD), BF16)
    svd[:PAD, :] = jnp.zeros((PAD, 2 * HD), BF16)
    svd[PAD + TOKENS :, :] = jnp.zeros((PAD, 2 * HD), BF16)
    hid[...] = jnp.zeros_like(hid)
    gup_ref[...] = jnp.zeros_like(gup_ref)
    slot_row = lax.broadcasted_iota(jnp.int32, (TOK, 3 * TOK), 0)
    slot_col = lax.broadcasted_iota(jnp.int32, (TOK, 3 * TOK), 1)
    expand[...] = jnp.where(slot_row - RANK == slot_col // TILE, 1.0, 0.0).astype(BF16)

    @pl.loop(0, N)
    def _(s):
        v_aug[rows(s), HD:] = jnp.ones((TOK, HD), BF16)
        high[rows(s), :] = jnp.full((TOK, HD), -1e30, F32)
        acc[rows(s), :] = jnp.zeros((TOK, 2 * HD), F32)

    load_x.wait()
    load_dw.wait()
    load_up.wait()
    mask_row = lax.broadcasted_iota(jnp.int32, (DROWS - RANK, TOK), 0)
    mask_col = lax.broadcasted_iota(jnp.int32, (DROWS - RANK, TOK), 1)
    mask = jnp.zeros((DROWS - RANK, TOK), F32)
    for slot in range(6):
        wanted = (me - 1) * 2 + slot
        seen = []
        for t in range(2):
            hit = jnp.float32(0.0)
            for e in range(4):
                hit = jnp.where(nb_ref[t, e] == wanted, jnp.float32(1.0), hit)
            seen.append(hit)
        mask = jnp.where(
            mask_row == slot, jnp.where(mask_col < TILE, seen[0], seen[1]), mask
        )
    dbuf[lane, z, :RANK, :] = dot_tt(dwbuf[...], xbuf[...], ((1,), (1,))).astype(BF16)
    dbuf[lane, z, RANK:, :] = mask.astype(BF16)

    pl.semaphore_wait(barrier, N - 1)

    @pl.loop(1, NZ)
    def _(j):
        remote(
            dbuf.at[lane, z],
            dbuf.at[lane, z],
            dsem_s.at[0],
            dsem_a,
            device(y, lax.rem(z + ring_step(j), NZ), c),
        ).start()

    def send_all(*arrays):
        @pl.loop(1, N)
        def _(i):
            target = device(
                lax.rem(y + lax.rem(i // 2, 2), 2),
                lax.rem(z + ring_step(i // 4), NZ),
                lax.rem(c + lax.rem(i, 2), 2),
            )
            for hbm, buf, send, sems in arrays:
                remote(
                    hbm.at[:, cols(target)], buf.at[rows(me)], send, sems.at[me], target
                ).start()

    send_all((q_hbm, qbuf, ssem.at[0], qsem))

    drain(dbuf.at[0, pl.ds(0, NZ - 1)], dsem_a)
    for dy, dc in ((0, 1), (1, 0), (1, 1)):
        remote(
            dbuf.at[lane],
            dbuf.at[lane],
            dsem_s.at[1],
            dsem_b.at[lane],
            device(lax.rem(y + dy, 2), z, lax.rem(c + dc, 2)),
        ).start()

    send_all((k_hbm, kbuf, ssem.at[1], ksem), (v_hbm, vbuf, ssem.at[2], vsem))

    for dy, dc in ((0, 1), (1, 0), (1, 1)):
        other = lax.rem(y + dy, 2) * 2 + lax.rem(c + dc, 2)
        drain(dbuf.at[other], dsem_b.at[other])

    @pl.loop(0, N)
    def _(s):
        drain(qbuf.at[rows(s)], qsem.at[s])

    def position(j):
        return lax.rem(z + NZ - ring_step(j), NZ)

    def send_out(j):
        s = device(lax.rem(j // 2, 2), position(j // 4), lax.rem(j, 2))

        @pl.when(s == me)
        def _():
            pltpu.make_async_copy(obuf.at[rows(s)], out_hbm.at[:, cols(me)], osem.at[2]).start()

        @pl.when(s != me)
        def _():
            remote(
                obuf.at[rows(s)], out_hbm.at[:, cols(me)], osem.at[0], osem.at[1], s
            ).start()

    def done(k):
        f = (k + 1) // 2
        return (2 * f - 3) * ((f + 2) // 4) + 3 * (k // NZ)

    @pl.loop(0, NZ)
    def _(g):
        place = position(g)
        for yy in range(2):
            for cc in range(2):
                s = device(yy, place, cc)
                drain(kbuf.at[rows(s)], ksem.at[s])
                keys_t[:, rows(s + 1)] = kbuf[rows(s), :].T
                block = jnp.concatenate(
                    [dbuf[yy * 2 + cc, place], jnp.zeros((TOK - DROWS, TOK), BF16)], axis=0
                ).T
                term = dot(block[:, :RANK], up_t[...])
                drain(vbuf.at[rows(s)], vsem.at[s])
                value = vbuf[rows(s), :]
                v_aug[rows(s), :HD] = value
                svd[rows(s + 1), :HD] = (value.astype(F32) + term).astype(BF16)
                svd[rows(s + 1), HD:] = block

        @pl.loop(done(g), done(g + 1))
        def _(j):
            if True:
                slabs = [device(at // 2, position(j), at % 2) for at in range(4)]
                seen = [dot(svd[rows(s + 1), HD:], expand[...]) for s in slabs]
                raw = [dot(qbuf[rows(s), :], keys_t[:, rows(s, 3 * TOK)]) for s in slabs]
                raw = [jnp.where(m > 0.5, r, -1e30) for m, r in zip(seen, raw)]
                most = [jnp.max(r, axis=1, keepdims=True) for r in raw]
                expo = [jnp.exp2((r - m) * EXP2_SCALE) for r, m in zip(raw, most)]
                norm = [1.0 / jnp.sum(e, axis=1, keepdims=True) for e in expo]
                weights = [(e * n).astype(BF16) for e, n in zip(expo, norm)]
                mixed = [dot(w, svd[rows(s, 3 * TOK), :]) for w, s in zip(weights, slabs)]
                for s, w, m in zip(slabs, weights, mixed):
                    wts[s] = w
                    stu[rows(s), :] = m[:, :HD]
                    obuf[rows(s), :] = m[:, :HD].astype(BF16)
                    mixd[rows(s), :] = m[:, HD:].astype(BF16)

        @pl.loop(4 * done(g), 4 * done(g + 1))
        def _(j):
            send_out(j)

        firsts = [(yy * NZ + place) * 2 for yy in range(2)]

        def score(i, scores, tops):
            block = pl.ds(pl.multiple_of(i * BQ, BQ), BQ)
            query = qbuf[block, :]
            top = high[block, :]
            for yy, first in enumerate(firsts):
                chunk = dot(query, keys_t[:, rows(first + 1, 2 * TOK)])
                scores[:, yy * 2 * TOK : (yy + 1) * 2 * TOK] = chunk
                top = jnp.maximum(top, jnp.maximum(chunk[:, :HD], chunk[:, HD:]))
            tops[...] = jnp.broadcast_to(jnp.max(top, axis=1, keepdims=True), (BQ, HD))

        def update(i, scores, tops):
            block = pl.ds(pl.multiple_of(i * BQ, BQ), BQ)
            new = tops[...]
            alpha = jnp.exp2((high[block, :] - new) * EXP2_SCALE)
            high[block, :] = new
            part = None
            for yy, first in enumerate(firsts):
                expo = jnp.concatenate(
                    [
                        jnp.exp2(
                            (scores[:, (2 * yy + h) * HD : (2 * yy + h + 1) * HD] - new)
                            * EXP2_SCALE
                        ).astype(BF16)
                        for h in range(2)
                    ],
                    axis=1,
                )
                term = dot(expo, v_aug[rows(first, 2 * TOK), :])
                part = term if part is None else part + term
            acc[block, :HD] = acc[block, :HD] * alpha + part[:, :HD]
            acc[block, HD:] = acc[block, HD:] * alpha + part[:, HD:]

        blocks = TOKENS // BQ
        score(0, scores0, tops0)

        @pl.loop(0, blocks // 2 - 1)
        def _(i):
            update(2 * i, scores0, tops0)
            score(2 * i + 1, scores1, tops1)
            update(2 * i + 1, scores1, tops1)
            score(2 * i + 2, scores0, tops0)

        update(blocks - 2, scores0, tops0)
        score(blocks - 1, scores1, tops1)
        update(blocks - 1, scores1, tops1)

    def block(src, offset, owner):
        return src[:, pl.ds(pl.multiple_of(offset + owner * TOK, TOK), TOK)]

    def exchange(k, src, offset, ch):
        for m in range(4):
            owner = 4 * ch + m
            rs_s1[k, owner] = block(src, offset, 2 * owner + 1 - c).astype(BF16)
        part = pl.ds(4 * ch, 4)
        remote(
            rs_s1.at[k, part], rs_r1.at[k, part], rs_sem.at[k, 0], rs_pair.at[k, ch], me + 1 - 2 * c
        ).start()

    def chip_at(i):
        r = N // 2 - 1 - i
        return lax.rem(y + lax.rem(r, 2), 2) * NZ + lax.rem(z + ring_step(r // 2), NZ)

    def scatter(k, src, offset):
        @pl.loop(0, 4)
        def _(ch):
            drain(rs_r1.at[k, pl.ds(4 * ch, 4)], rs_pair.at[k, ch])
            for m in range(4):
                owner = 4 * ch + m
                rs_s2[k, owner] = (
                    block(src, offset, 2 * owner + c) + rs_r1[k, owner].astype(F32)
                ).astype(BF16)

        @pl.loop(0, N // 2 - 1)
        def _(i):
            owner = chip_at(i)
            remote(
                rs_s2.at[k, owner], rs_r2.at[k, chip], rs_sem.at[k, 1], rs_sem.at[k, 2], 2 * owner + c
            ).start()

        rs_r2[k, chip] = rs_s2[k, chip]

    def total(k):
        drain(rs_r2.at[k, pl.ds(0, N // 2 - 1)], rs_sem.at[k, 2])
        result = rs_r2[k, 0].astype(F32)
        for m in range(1, N // 2):
            result = result + rs_r2[k, m].astype(F32)
        return result

    @pl.loop(0, 4)
    def _(ch):
        @pl.loop(0, 2)
        def _(h):
            slabs = [8 * ch + 4 * h + u for u in range(4)]
            span = rows(slabs[0], 4 * TOK)
            teacher = (acc[span, :HD] / acc[span, HD:]).astype(BF16).astype(F32)
            grad = ((stu[span, :] - teacher) * (TOKENS**-0.5)).astype(BF16)
            latent = dot_tt(up_t[...], grad, ((1,), (1,))).astype(BF16)
            terms = [dot(latent[:, u * TOK : (u + 1) * TOK], wts[s]) for u, s in enumerate(slabs)]
            for s, term in zip(slabs, terms):
                hid[:, rows(s, 3 * TOK)] += term
            gup_ref[...] += dot_tt(mixd[span, :RANK], grad, ((0,), (0,)))

        @pl.when(ch > 0)
        def _():
            exchange(0, hid, PAD, ch - 1)

    exchange(0, hid, PAD, 3)


    scatter(0, hid, PAD)

    hidden = total(0)
    hid_hi[...] = hidden.astype(BF16)
    hid_lo[...] = (hidden - hidden.astype(BF16).astype(F32)).astype(BF16)

    def forward(n):
        drain(rs_r1.at[1, pl.ds(4 * n, 4)], rs_pair.at[1, n])
        for u in range(4):
            i = 4 * n + u
            rs_s2[1, i] = (block(gdn, 0, 2 * i + c) + rs_r1[1, i].astype(F32)).astype(BF16)
        for u in range(4):
            i = 4 * n + u

            @pl.when(i < N // 2 - 1)
            def _():
                remote(
                    rs_s2.at[1, i],
                    rs_r2.at[1, i],
                    rs_sem.at[1, 1],
                    rs_sem.at[1, 2],
                    2 * chip_at(i) + c,
                ).start()

    @pl.loop(0, 4)
    def _(n):
        for u in range(4):
            i = 4 * n + u
            feed = xbuf[:, rows(2 * chip_at(i), 2 * TOK)]
            gdn[:, rows(2 * i, 2 * TOK)] = dot(hid_hi[...], feed) + dot(hid_lo[...], feed)
        exchange(1, gdn, 0, n)

        @pl.when(n > 0)
        def _():
            forward(n - 1)

    forward(3)
    rs_r2[1, N // 2 - 1] = rs_s2[1, N // 2 - 1]
    gdown_ref[...] = total(1)

    for a in range(3):
        drain(kbuf.at[pl.ds(0, (N - 1) * TOK)], ssem.at[a])
    drain(dbuf.at[0, pl.ds(0, NZ - 1)], dsem_s.at[0])
    drain(dbuf.at[pl.ds(0, 3)], dsem_s.at[1])
    for k in range(2):
        drain(rs_s1.at[k], rs_sem.at[k, 0])
        drain(rs_s2.at[k, pl.ds(0, N // 2 - 1)], rs_sem.at[k, 1])
    drain(obuf.at[pl.ds(0, (N - 1) * TOK)], osem.at[0])
    drain(obuf.at[pl.ds(0, (N - 1) * TOK)], osem.at[1])
    drain(obuf.at[pl.ds(0, TOK)], osem.at[2])


def local(
    queries, keys, values, value_layer_input, adapter_down_weight, adapter_up_weight, neighbors
):
    anywhere = pl.BlockSpec(memory_space=pl.ANY)
    vmem = pl.BlockSpec(memory_space=pltpu.VMEM)
    dma = pltpu.SemaphoreType.DMA
    student_out, grad_down, grad_up = pl.pallas_call(
        kernel,
        out_shape=(
            pltpu.VMEM((TOK, WIDTH), BF16),
            pltpu.VMEM((RANK, HD), F32),
            pltpu.VMEM((RANK, HD), F32),
        ),
        in_specs=[anywhere] * 6 + [pl.BlockSpec(memory_space=pltpu.SMEM)],
        out_specs=(vmem, vmem, vmem),
        scratch_shapes=[
            pltpu.VMEM((TOK, WIDTH), BF16),
            pltpu.VMEM((RANK, WIDTH), BF16),
            pltpu.VMEM((RANK, HD), BF16),
            pltpu.VMEM((TOKENS, HD), BF16),
            pltpu.VMEM((TOKENS, HD), BF16),
            pltpu.VMEM((TOKENS, HD), BF16),
            pltpu.VMEM((HD, TOKENS + 2 * PAD), BF16),
            pltpu.VMEM((TOKENS, 2 * HD), BF16),
            pltpu.VMEM((TOKENS + 2 * PAD, 2 * HD), BF16),
            pltpu.VMEM((TOK, 3 * TOK), BF16),
            pltpu.VMEM((BQ, CK), F32),
            pltpu.VMEM((BQ, CK), F32),
            pltpu.VMEM((BQ, HD), F32),
            pltpu.VMEM((BQ, HD), F32),
            pltpu.VMEM((TOKENS, HD), F32),
            pltpu.VMEM((TOKENS, 2 * HD), F32),
            pltpu.VMEM((N, TOK, 3 * TOK), BF16),
            pltpu.VMEM((TOKENS, HD), F32),
            pltpu.VMEM((TOKENS, HD), BF16),
            pltpu.VMEM((TOKENS, HD), BF16),
            pltpu.VMEM((4, NZ, DROWS, TOK), BF16),
            pltpu.VMEM((RANK, TOKENS + 2 * PAD), F32),
            pltpu.VMEM((RANK, WIDTH), F32),
            pltpu.VMEM((RANK, TOK), BF16),
            pltpu.VMEM((RANK, TOK), BF16),
            pltpu.VMEM((2, N // 2, RANK, TOK), BF16),
            pltpu.VMEM((2, N // 2, RANK, TOK), BF16),
            pltpu.VMEM((2, N // 2, RANK, TOK), BF16),
            pltpu.VMEM((2, N // 2, RANK, TOK), BF16),
            dma((3,)),
            dma((3,)),
            dma((N,)),
            dma((N,)),
            dma((N,)),
            dma((3,)),
            dma((2,)),
            dma,
            dma((4,)),
            dma((2, 3)),
            dma((2, 4)),
        ],
        compiler_params=pltpu.CompilerParams(
            collective_id=0, has_side_effects=True, vmem_limit_bytes=60 << 20
        ),
    )(
        queries,
        keys,
        values,
        value_layer_input,
        adapter_down_weight.T,
        adapter_up_weight.T,
        neighbors,
    )
    return student_out, grad_down.T, grad_up.T


def solution(mesh):
    rows_split = P(("video", "context"), None)
    return jax.shard_map(
        local,
        mesh=mesh,
        in_specs=(rows_split,) * 4 + (P(), P(), rows_split),
        out_specs=(rows_split,) * 3,
        check_vma=False,
    )
```

```python
import math

import jax
import jax.numpy as jnp
from jax import lax
from jax.experimental import pallas as pl
from jax.experimental.pallas import tpu as pltpu
from jax.sharding import PartitionSpec as P

MESH = pl.DeviceIdType.MESH
F32 = jnp.float32
BF16 = jnp.bfloat16

N = 32
NZ = 8
TOK = 128
HD = 128
RANK = 64
TILE = 64
TOKENS = N * TOK
WIDTH = N * HD
PAD = TOK
DROWS = 80
BQ = 4 * TOK
CK = 4 * TOK
EXP2_SCALE = math.log2(math.e) / math.sqrt(HD)


def ring_step(j):
    half = (j + 1) // 2
    return lax.rem(half * lax.rem(j, 2) + (NZ - half) * (1 - lax.rem(j, 2)), NZ)


def dot(a, b):
    return jnp.dot(a, b, preferred_element_type=F32)


def dot_tt(a, b, dims):
    return lax.dot_general(a, b, (dims, ((), ())), preferred_element_type=F32)


def kernel(
    q_hbm,
    k_hbm,
    v_hbm,
    x_hbm,
    down_hbm,
    up_hbm,
    nb_ref,
    out_hbm,
    gdown_ref,
    gup_ref,
    xbuf,
    dwbuf,
    up_t,
    kbuf,
    vbuf,
    qbuf,
    keys_t,
    v_aug,
    svd,
    expand,
    scores0,
    scores1,
    tops0,
    tops1,
    high,
    acc,
    wts,
    stu,
    mixd,
    obuf,
    dbuf,
    hid,
    gdn,
    hid_hi,
    hid_lo,
    rs_s1,
    rs_r1,
    rs_s2,
    rs_r2,
    load_sem,
    ssem,
    ksem,
    vsem,
    qsem,
    osem,
    dsem_s,
    dsem_a,
    dsem_b,
    rs_sem,
    rs_pair,
):
    me = lax.axis_index("context")
    y, z, c = me // 16, lax.rem(me // 2, NZ), lax.rem(me, 2)
    chip = me // 2
    lane = y * 2 + c

    def device(yy, zz, cc):
        return (yy * NZ + zz) * 2 + cc

    def remote(src, dst, send, recv, target):
        return pltpu.make_async_remote_copy(
            src_ref=src,
            dst_ref=dst,
            send_sem=send,
            recv_sem=recv,
            device_id={"context": target},
            device_id_type=MESH,
        )

    def cols(index):
        return pl.ds(pl.multiple_of(index * HD, HD), HD)

    def rows(index, count=TOK):
        return pl.ds(pl.multiple_of(index * TOK, TOK), count)

    def drain(ref, sem):
        pltpu.make_async_copy(ref, ref, sem).wait()

    load_x = pltpu.make_async_copy(x_hbm, xbuf, load_sem.at[0])
    load_dw = pltpu.make_async_copy(down_hbm, dwbuf, load_sem.at[1])
    load_up = pltpu.make_async_copy(up_hbm.at[:, cols(me)], up_t, load_sem.at[2])
    load_x.start()
    load_dw.start()
    load_up.start()

    barrier = pltpu.get_barrier_semaphore()

    @pl.loop(1, N)
    def _(j):
        pl.semaphore_signal(
            barrier, inc=1, device_id={"context": lax.rem(me + j, N)}, device_id_type=MESH
        )

    for hbm, buf, sems in ((k_hbm, kbuf, ksem), (v_hbm, vbuf, vsem), (q_hbm, qbuf, qsem)):
        pltpu.make_async_copy(hbm.at[:, cols(me)], buf.at[rows(me)], sems.at[me]).start()

    keys_t[:, :PAD] = jnp.zeros((HD, PAD), BF16)
    keys_t[:, PAD + TOKENS :] = jnp.zeros((HD, PAD), BF16)
    svd[:PAD, :] = jnp.zeros((PAD, 2 * HD), BF16)
    svd[PAD + TOKENS :, :] = jnp.zeros((PAD, 2 * HD), BF16)
    hid[...] = jnp.zeros_like(hid)
    gup_ref[...] = jnp.zeros_like(gup_ref)
    slot_row = lax.broadcasted_iota(jnp.int32, (TOK, 3 * TOK), 0)
    slot_col = lax.broadcasted_iota(jnp.int32, (TOK, 3 * TOK), 1)
    expand[...] = jnp.where(slot_row - RANK == slot_col // TILE, 1.0, 0.0).astype(BF16)

    @pl.loop(0, N)
    def _(s):
        v_aug[rows(s), HD:] = jnp.ones((TOK, HD), BF16)
        high[rows(s), :] = jnp.full((TOK, HD), -1e30, F32)
        acc[rows(s), :] = jnp.zeros((TOK, 2 * HD), F32)

    load_x.wait()
    load_dw.wait()
    load_up.wait()
    mask_row = lax.broadcasted_iota(jnp.int32, (DROWS - RANK, TOK), 0)
    mask_col = lax.broadcasted_iota(jnp.int32, (DROWS - RANK, TOK), 1)
    mask = jnp.zeros((DROWS - RANK, TOK), F32)
    for slot in range(6):
        wanted = (me - 1) * 2 + slot
        seen = []
        for t in range(2):
            hit = jnp.float32(0.0)
            for e in range(4):
                hit = jnp.where(nb_ref[t, e] == wanted, jnp.float32(1.0), hit)
            seen.append(hit)
        mask = jnp.where(
            mask_row == slot, jnp.where(mask_col < TILE, seen[0], seen[1]), mask
        )
    dbuf[lane, z, :RANK, :] = dot_tt(dwbuf[...], xbuf[...], ((1,), (1,))).astype(BF16)
    dbuf[lane, z, RANK:, :] = mask.astype(BF16)

    pl.semaphore_wait(barrier, N - 1)

    @pl.loop(1, NZ)
    def _(j):
        remote(
            dbuf.at[lane, z],
            dbuf.at[lane, z],
            dsem_s.at[0],
            dsem_a,
            device(y, lax.rem(z + ring_step(j), NZ), c),
        ).start()

    def send_all(*arrays):
        @pl.loop(1, N)
        def _(i):
            target = device(
                lax.rem(y + lax.rem(i // 2, 2), 2),
                lax.rem(z + ring_step(i // 4), NZ),
                lax.rem(c + lax.rem(i, 2), 2),
            )
            for hbm, buf, send, sems in arrays:
                remote(
                    hbm.at[:, cols(target)], buf.at[rows(me)], send, sems.at[me], target
                ).start()

    send_all((q_hbm, qbuf, ssem.at[0], qsem))

    drain(dbuf.at[0, pl.ds(0, NZ - 1)], dsem_a)
    for dy, dc in ((0, 1), (1, 0), (1, 1)):
        remote(
            dbuf.at[lane],
            dbuf.at[lane],
            dsem_s.at[1],
            dsem_b.at[lane],
            device(lax.rem(y + dy, 2), z, lax.rem(c + dc, 2)),
        ).start()

    send_all((k_hbm, kbuf, ssem.at[1], ksem), (v_hbm, vbuf, ssem.at[2], vsem))

    for dy, dc in ((0, 1), (1, 0), (1, 1)):
        other = lax.rem(y + dy, 2) * 2 + lax.rem(c + dc, 2)
        drain(dbuf.at[other], dsem_b.at[other])

    @pl.loop(0, N)
    def _(s):
        drain(qbuf.at[rows(s)], qsem.at[s])

    def position(j):
        return lax.rem(z + NZ - ring_step(j), NZ)

    def student_slab(j):
        quad, at = j // 4, lax.rem(j, 4)
        far, outer, side = (quad + 1) // 2, lax.rem(quad + 1, 2), lax.rem(at, 2)
        return device(
            at // 2,
            lax.rem(z + NZ + (2 * side - 1) * far, NZ),
            (1 - side) * (1 - outer) + side * outer,
        )

    def send_out(quad):
        @pl.loop(4 * quad, 4 * quad + 4)
        def _(j):
            s = student_slab(j)

            @pl.when(s == me)
            def _():
                pltpu.make_async_copy(
                    obuf.at[rows(s)], out_hbm.at[:, cols(me)], osem.at[2]
                ).start()

            @pl.when(s != me)
            def _():
                remote(
                    obuf.at[rows(s)], out_hbm.at[:, cols(me)], osem.at[0], osem.at[1], s
                ).start()

    def done(k):
        f = (k + 1) // 2
        return (2 * f - 2) * ((f + 2) // 4) + 2 * (k // NZ)

    @pl.loop(0, NZ)
    def _(g):
        place = position(g)
        for yy in range(2):
            for cc in range(2):
                s = device(yy, place, cc)
                drain(kbuf.at[rows(s)], ksem.at[s])
                keys_t[:, rows(s + 1)] = kbuf[rows(s), :].T
                block = jnp.concatenate(
                    [dbuf[yy * 2 + cc, place], jnp.zeros((TOK - DROWS, TOK), BF16)], axis=0
                ).T
                term = dot(block[:, :RANK], up_t[...])
                drain(vbuf.at[rows(s)], vsem.at[s])
                value = vbuf[rows(s), :]
                v_aug[rows(s), :HD] = value
                svd[rows(s + 1), :HD] = (value.astype(F32) + term).astype(BF16)
                svd[rows(s + 1), HD:] = block

        @pl.loop(done(g), done(g + 1))
        def _(j):
            slabs = [student_slab(4 * j + at) for at in range(4)]
            seen = [dot(svd[rows(s + 1), HD:], expand[...]) for s in slabs]
            raw = [dot(qbuf[rows(s), :], keys_t[:, rows(s, 3 * TOK)]) for s in slabs]
            raw = [jnp.where(m > 0.5, r, -1e30) for m, r in zip(seen, raw)]
            most = [jnp.max(r, axis=1, keepdims=True) for r in raw]
            expo = [jnp.exp2((r - m) * EXP2_SCALE) for r, m in zip(raw, most)]
            norm = [1.0 / jnp.sum(e, axis=1, keepdims=True) for e in expo]
            weights = [(e * n).astype(BF16) for e, n in zip(expo, norm)]
            mixed = [dot(w, svd[rows(s, 3 * TOK), :]) for w, s in zip(weights, slabs)]
            for s, w, m in zip(slabs, weights, mixed):
                wts[s] = w
                stu[rows(s), :] = m[:, :HD]
                obuf[rows(s), :] = m[:, :HD].astype(BF16)
                mixd[rows(s), :] = m[:, HD:].astype(BF16)

            @pl.when(j > done(g))
            def _():
                send_out(j - 1)

        firsts = [(yy * NZ + place) * 2 for yy in range(2)]

        def score(i, scores, tops):
            block = pl.ds(pl.multiple_of(i * BQ, BQ), BQ)
            query = qbuf[block, :]
            top = high[block, :]
            for yy, first in enumerate(firsts):
                chunk = dot(query, keys_t[:, rows(first + 1, 2 * TOK)])
                scores[:, yy * 2 * TOK : (yy + 1) * 2 * TOK] = chunk
                top = jnp.maximum(top, jnp.maximum(chunk[:, :HD], chunk[:, HD:]))
            tops[...] = jnp.broadcast_to(jnp.max(top, axis=1, keepdims=True), (BQ, HD))

        def update(i, scores, tops):
            block = pl.ds(pl.multiple_of(i * BQ, BQ), BQ)
            new = tops[...]
            alpha = jnp.exp2((high[block, :] - new) * EXP2_SCALE)
            high[block, :] = new
            part = None
            for yy, first in enumerate(firsts):
                expo = jnp.concatenate(
                    [
                        jnp.exp2(
                            (scores[:, (2 * yy + h) * HD : (2 * yy + h + 1) * HD] - new)
                            * EXP2_SCALE
                        ).astype(BF16)
                        for h in range(2)
                    ],
                    axis=1,
                )
                term = dot(expo, v_aug[rows(first, 2 * TOK), :])
                part = term if part is None else part + term
            acc[block, :HD] = acc[block, :HD] * alpha + part[:, :HD]
            acc[block, HD:] = acc[block, HD:] * alpha + part[:, HD:]

        blocks = TOKENS // BQ
        score(0, scores0, tops0)

        @pl.when(done(g + 1) > done(g))
        def _():
            send_out(done(g + 1) - 1)


        @pl.loop(0, blocks // 2 - 1)
        def _(i):
            update(2 * i, scores0, tops0)
            score(2 * i + 1, scores1, tops1)
            update(2 * i + 1, scores1, tops1)
            score(2 * i + 2, scores0, tops0)

        update(blocks - 2, scores0, tops0)
        score(blocks - 1, scores1, tops1)
        update(blocks - 1, scores1, tops1)

    def block(src, offset, owner):
        return src[:, pl.ds(pl.multiple_of(offset + owner * TOK, TOK), TOK)]

    def exchange(k, src, offset, ch):
        for m in range(4):
            owner = 4 * ch + m
            rs_s1[k, owner] = block(src, offset, 2 * owner + 1 - c).astype(BF16)
        part = pl.ds(4 * ch, 4)
        remote(
            rs_s1.at[k, part], rs_r1.at[k, part], rs_sem.at[k, 0], rs_pair.at[k, ch], me + 1 - 2 * c
        ).start()

    def chip_at(i):
        r = N // 2 - 1 - i
        return lax.rem(y + lax.rem(r, 2), 2) * NZ + lax.rem(z + ring_step(r // 2), NZ)

    def scatter(k, src, offset):
        @pl.loop(0, 4)
        def _(ch):
            drain(rs_r1.at[k, pl.ds(4 * ch, 4)], rs_pair.at[k, ch])
            for m in range(4):
                owner = 4 * ch + m
                rs_s2[k, owner] = (
                    block(src, offset, 2 * owner + c) + rs_r1[k, owner].astype(F32)
                ).astype(BF16)

        @pl.loop(0, N // 2 - 1)
        def _(i):
            owner = chip_at(i)
            remote(
                rs_s2.at[k, owner], rs_r2.at[k, chip], rs_sem.at[k, 1], rs_sem.at[k, 2], 2 * owner + c
            ).start()

        rs_r2[k, chip] = rs_s2[k, chip]

    def total(k):
        drain(rs_r2.at[k, pl.ds(0, N // 2 - 1)], rs_sem.at[k, 2])
        result = rs_r2[k, 0].astype(F32)
        for m in range(1, N // 2):
            result = result + rs_r2[k, m].astype(F32)
        return result

    @pl.loop(0, 4)
    def _(ch):
        @pl.loop(0, 2)
        def _(h):
            slabs = [8 * ch + 4 * h + u for u in range(4)]
            span = rows(slabs[0], 4 * TOK)
            teacher = (acc[span, :HD] / acc[span, HD:]).astype(BF16).astype(F32)
            grad = ((stu[span, :] - teacher) * (TOKENS**-0.5)).astype(BF16)
            latent = dot_tt(up_t[...], grad, ((1,), (1,))).astype(BF16)
            terms = [dot(latent[:, u * TOK : (u + 1) * TOK], wts[s]) for u, s in enumerate(slabs)]
            for s, term in zip(slabs, terms):
                hid[:, rows(s, 3 * TOK)] += term
            gup_ref[...] += dot_tt(mixd[span, :RANK], grad, ((0,), (0,)))

        @pl.when(ch > 0)
        def _():
            exchange(0, hid, PAD, ch - 1)

    exchange(0, hid, PAD, 3)


    scatter(0, hid, PAD)

    hidden = total(0)
    hid_hi[...] = hidden.astype(BF16)
    hid_lo[...] = (hidden - hidden.astype(BF16).astype(F32)).astype(BF16)

    def forward(n):
        drain(rs_r1.at[1, pl.ds(4 * n, 4)], rs_pair.at[1, n])
        for u in range(4):
            i = 4 * n + u
            rs_s2[1, i] = (block(gdn, 0, 2 * i + c) + rs_r1[1, i].astype(F32)).astype(BF16)
        for u in range(4):
            i = 4 * n + u

            @pl.when(i < N // 2 - 1)
            def _():
                remote(
                    rs_s2.at[1, i],
                    rs_r2.at[1, i],
                    rs_sem.at[1, 1],
                    rs_sem.at[1, 2],
                    2 * chip_at(i) + c,
                ).start()

    @pl.loop(0, 4)
    def _(n):
        for u in range(4):
            i = 4 * n + u
            feed = xbuf[:, rows(2 * chip_at(i), 2 * TOK)]
            gdn[:, rows(2 * i, 2 * TOK)] = dot(hid_hi[...], feed) + dot(hid_lo[...], feed)
        exchange(1, gdn, 0, n)

        @pl.when(n > 0)
        def _():
            forward(n - 1)

    forward(3)
    rs_r2[1, N // 2 - 1] = rs_s2[1, N // 2 - 1]
    gdown_ref[...] = total(1)

    for a in range(3):
        drain(kbuf.at[pl.ds(0, (N - 1) * TOK)], ssem.at[a])
    drain(dbuf.at[0, pl.ds(0, NZ - 1)], dsem_s.at[0])
    drain(dbuf.at[pl.ds(0, 3)], dsem_s.at[1])
    for k in range(2):
        drain(rs_s1.at[k], rs_sem.at[k, 0])
        drain(rs_s2.at[k, pl.ds(0, N // 2 - 1)], rs_sem.at[k, 1])
    drain(obuf.at[pl.ds(0, (N - 1) * TOK)], osem.at[0])
    drain(obuf.at[pl.ds(0, (N - 1) * TOK)], osem.at[1])
    drain(obuf.at[pl.ds(0, TOK)], osem.at[2])


def local(
    queries, keys, values, value_layer_input, adapter_down_weight, adapter_up_weight, neighbors
):
    anywhere = pl.BlockSpec(memory_space=pl.ANY)
    vmem = pl.BlockSpec(memory_space=pltpu.VMEM)
    dma = pltpu.SemaphoreType.DMA
    student_out, grad_down, grad_up = pl.pallas_call(
        kernel,
        out_shape=(
            pltpu.VMEM((TOK, WIDTH), BF16),
            pltpu.VMEM((RANK, HD), F32),
            pltpu.VMEM((RANK, HD), F32),
        ),
        in_specs=[anywhere] * 6 + [pl.BlockSpec(memory_space=pltpu.SMEM)],
        out_specs=(vmem, vmem, vmem),
        scratch_shapes=[
            pltpu.VMEM((TOK, WIDTH), BF16),
            pltpu.VMEM((RANK, WIDTH), BF16),
            pltpu.VMEM((RANK, HD), BF16),
            pltpu.VMEM((TOKENS, HD), BF16),
            pltpu.VMEM((TOKENS, HD), BF16),
            pltpu.VMEM((TOKENS, HD), BF16),
            pltpu.VMEM((HD, TOKENS + 2 * PAD), BF16),
            pltpu.VMEM((TOKENS, 2 * HD), BF16),
            pltpu.VMEM((TOKENS + 2 * PAD, 2 * HD), BF16),
            pltpu.VMEM((TOK, 3 * TOK), BF16),
            pltpu.VMEM((BQ, CK), F32),
            pltpu.VMEM((BQ, CK), F32),
            pltpu.VMEM((BQ, HD), F32),
            pltpu.VMEM((BQ, HD), F32),
            pltpu.VMEM((TOKENS, HD), F32),
            pltpu.VMEM((TOKENS, 2 * HD), F32),
            pltpu.VMEM((N, TOK, 3 * TOK), BF16),
            pltpu.VMEM((TOKENS, HD), F32),
            pltpu.VMEM((TOKENS, HD), BF16),
            pltpu.VMEM((TOKENS, HD), BF16),
            pltpu.VMEM((4, NZ, DROWS, TOK), BF16),
            pltpu.VMEM((RANK, TOKENS + 2 * PAD), F32),
            pltpu.VMEM((RANK, WIDTH), F32),
            pltpu.VMEM((RANK, TOK), BF16),
            pltpu.VMEM((RANK, TOK), BF16),
            pltpu.VMEM((2, N // 2, RANK, TOK), BF16),
            pltpu.VMEM((2, N // 2, RANK, TOK), BF16),
            pltpu.VMEM((2, N // 2, RANK, TOK), BF16),
            pltpu.VMEM((2, N // 2, RANK, TOK), BF16),
            dma((3,)),
            dma((3,)),
            dma((N,)),
            dma((N,)),
            dma((N,)),
            dma((3,)),
            dma((2,)),
            dma,
            dma((4,)),
            dma((2, 3)),
            dma((2, 4)),
        ],
        compiler_params=pltpu.CompilerParams(
            collective_id=0, has_side_effects=True, vmem_limit_bytes=60 << 20
        ),
    )(
        queries,
        keys,
        values,
        value_layer_input,
        adapter_down_weight.T,
        adapter_up_weight.T,
        neighbors,
    )
    return student_out, grad_down.T, grad_up.T


def solution(mesh):
    rows_split = P(("video", "context"), None)
    return jax.shard_map(
        local,
        mesh=mesh,
        in_specs=(rows_split,) * 4 + (P(), P(), rows_split),
        out_specs=(rows_split,) * 3,
        check_vma=False,
    )
```

```python
import math

import jax
import jax.numpy as jnp
from jax import lax
from jax.experimental import pallas as pl
from jax.experimental.pallas import tpu as pltpu
from jax.sharding import PartitionSpec as P

MESH = pl.DeviceIdType.MESH
F32 = jnp.float32
BF16 = jnp.bfloat16

N = 32
NZ = 8
TOK = 128
HD = 128
RANK = 64
TILE = 64
TOKENS = N * TOK
WIDTH = N * HD
PAD = TOK
DROWS = 80
BQ = 4 * TOK
CK = 4 * TOK
EXP2_SCALE = math.log2(math.e) / math.sqrt(HD)


def ring_step(j):
    half = (j + 1) // 2
    return lax.rem(half * lax.rem(j, 2) + (NZ - half) * (1 - lax.rem(j, 2)), NZ)


def dot(a, b):
    return jnp.dot(a, b, preferred_element_type=F32)


def dot_tt(a, b, dims):
    return lax.dot_general(a, b, (dims, ((), ())), preferred_element_type=F32)


def kernel(
    q_hbm,
    k_hbm,
    v_hbm,
    x_hbm,
    down_hbm,
    up_hbm,
    nb_ref,
    out_hbm,
    gdown_ref,
    gup_ref,
    xbuf,
    dwbuf,
    up_t,
    kbuf,
    vbuf,
    qbuf,
    keys_t,
    v_aug,
    svd,
    expand,
    scores0,
    scores1,
    tops0,
    tops1,
    high,
    acc,
    wts,
    stu,
    mixd,
    obuf,
    dbuf,
    hid,
    gdn,
    hid_hi,
    hid_lo,
    rs_s1,
    rs_r1,
    rs_s2,
    rs_r2,
    load_sem,
    ssem,
    ksem,
    vsem,
    qsem,
    osem,
    dsem_s,
    dsem_a,
    dsem_b,
    rs_sem,
    rs_pair,
):
    me = lax.axis_index("context")
    y, z, c = me // 16, lax.rem(me // 2, NZ), lax.rem(me, 2)
    chip = me // 2
    lane = y * 2 + c

    def device(yy, zz, cc):
        return (yy * NZ + zz) * 2 + cc

    def remote(src, dst, send, recv, target):
        return pltpu.make_async_remote_copy(
            src_ref=src,
            dst_ref=dst,
            send_sem=send,
            recv_sem=recv,
            device_id={"context": target},
            device_id_type=MESH,
        )

    def cols(index):
        return pl.ds(pl.multiple_of(index * HD, HD), HD)

    def rows(index, count=TOK):
        return pl.ds(pl.multiple_of(index * TOK, TOK), count)

    def drain(ref, sem):
        pltpu.make_async_copy(ref, ref, sem).wait()

    load_x = pltpu.make_async_copy(x_hbm, xbuf, load_sem.at[0])
    load_dw = pltpu.make_async_copy(down_hbm, dwbuf, load_sem.at[1])
    load_up = pltpu.make_async_copy(up_hbm.at[:, cols(me)], up_t, load_sem.at[2])
    load_x.start()
    load_dw.start()
    load_up.start()

    barrier = pltpu.get_barrier_semaphore()

    @pl.loop(1, N)
    def _(j):
        pl.semaphore_signal(
            barrier, inc=1, device_id={"context": lax.rem(me + j, N)}, device_id_type=MESH
        )

    for hbm, buf, sems in ((k_hbm, kbuf, ksem), (v_hbm, vbuf, vsem), (q_hbm, qbuf, qsem)):
        pltpu.make_async_copy(hbm.at[:, cols(me)], buf.at[rows(me)], sems.at[me]).start()

    keys_t[:, :PAD] = jnp.zeros((HD, PAD), BF16)
    keys_t[:, PAD + TOKENS :] = jnp.zeros((HD, PAD), BF16)
    svd[:PAD, :] = jnp.zeros((PAD, 2 * HD), BF16)
    svd[PAD + TOKENS :, :] = jnp.zeros((PAD, 2 * HD), BF16)
    hid[...] = jnp.zeros_like(hid)
    gup_ref[...] = jnp.zeros_like(gup_ref)
    slot_row = lax.broadcasted_iota(jnp.int32, (TOK, 3 * TOK), 0)
    slot_col = lax.broadcasted_iota(jnp.int32, (TOK, 3 * TOK), 1)
    expand[...] = jnp.where(slot_row - RANK == slot_col // TILE, 1.0, 0.0).astype(BF16)

    @pl.loop(0, N)
    def _(s):
        v_aug[rows(s), HD:] = jnp.ones((TOK, HD), BF16)
        high[rows(s), :] = jnp.full((TOK, HD), -1e30, F32)
        acc[rows(s), :] = jnp.zeros((TOK, 2 * HD), F32)

    load_x.wait()
    load_dw.wait()
    load_up.wait()
    mask_row = lax.broadcasted_iota(jnp.int32, (DROWS - RANK, TOK), 0)
    mask_col = lax.broadcasted_iota(jnp.int32, (DROWS - RANK, TOK), 1)
    mask = jnp.zeros((DROWS - RANK, TOK), F32)
    for slot in range(6):
        wanted = (me - 1) * 2 + slot
        seen = []
        for t in range(2):
            hit = jnp.float32(0.0)
            for e in range(4):
                hit = jnp.where(nb_ref[t, e] == wanted, jnp.float32(1.0), hit)
            seen.append(hit)
        mask = jnp.where(
            mask_row == slot, jnp.where(mask_col < TILE, seen[0], seen[1]), mask
        )
    dbuf[lane, z, :RANK, :] = dot_tt(dwbuf[...], xbuf[...], ((1,), (1,))).astype(BF16)
    dbuf[lane, z, RANK:, :] = mask.astype(BF16)

    pl.semaphore_wait(barrier, N - 1)

    @pl.loop(1, NZ)
    def _(j):
        remote(
            dbuf.at[lane, z],
            dbuf.at[lane, z],
            dsem_s.at[0],
            dsem_a,
            device(y, lax.rem(z + ring_step(j), NZ), c),
        ).start()

    def send_all(*arrays):
        @pl.loop(0, N)
        def _(i):
            far, w = (i + 4) // NZ, lax.rem(i + 4, NZ)
            side = lax.rem(w, 2)
            target = device(
                lax.rem(y + lax.rem(w // 2, 2), 2),
                lax.rem(z + NZ + (1 - 2 * side) * far, NZ),
                lax.rem(c + w // 4 + side, 2),
            )

            @pl.when(target != me)
            def _():
                for hbm, buf, send, sems in arrays:
                    remote(
                        hbm.at[:, cols(target)], buf.at[rows(me)], send, sems.at[me], target
                    ).start()

    send_all((q_hbm, qbuf, ssem.at[0], qsem))

    drain(dbuf.at[0, pl.ds(0, NZ - 1)], dsem_a)
    for dy, dc in ((0, 1), (1, 0), (1, 1)):
        remote(
            dbuf.at[lane],
            dbuf.at[lane],
            dsem_s.at[1],
            dsem_b.at[lane],
            device(lax.rem(y + dy, 2), z, lax.rem(c + dc, 2)),
        ).start()

    send_all((k_hbm, kbuf, ssem.at[1], ksem), (v_hbm, vbuf, ssem.at[2], vsem))

    for dy, dc in ((0, 1), (1, 0), (1, 1)):
        other = lax.rem(y + dy, 2) * 2 + lax.rem(c + dc, 2)
        drain(dbuf.at[other], dsem_b.at[other])

    @pl.loop(0, N)
    def _(s):
        drain(qbuf.at[rows(s)], qsem.at[s])

    def position(j):
        return lax.rem(z + NZ - ring_step(j), NZ)

    def student_slab(j):
        quad, at = j // 4, lax.rem(j, 4)
        far, outer, side = (quad + 1) // 2, lax.rem(quad + 1, 2), lax.rem(at, 2)
        return device(
            at // 2,
            lax.rem(z + NZ + (2 * side - 1) * far, NZ),
            (1 - side) * (1 - outer) + side * outer,
        )

    def send_out(quad):
        @pl.loop(4 * quad, 4 * quad + 4)
        def _(j):
            s = student_slab(j)

            @pl.when(s == me)
            def _():
                pltpu.make_async_copy(
                    obuf.at[rows(s)], out_hbm.at[:, cols(me)], osem.at[2]
                ).start()

            @pl.when(s != me)
            def _():
                remote(
                    obuf.at[rows(s)], out_hbm.at[:, cols(me)], osem.at[0], osem.at[1], s
                ).start()

    def done(k):
        f = (k + 1) // 2
        return (2 * f - 2) * ((f + 2) // 4) + 2 * (k // NZ)

    @pl.loop(0, NZ)
    def _(g):
        place = position(g)
        for yy in range(2):
            for cc in range(2):
                s = device(yy, place, cc)
                drain(kbuf.at[rows(s)], ksem.at[s])
                keys_t[:, rows(s + 1)] = kbuf[rows(s), :].T
                block = jnp.concatenate(
                    [dbuf[yy * 2 + cc, place], jnp.zeros((TOK - DROWS, TOK), BF16)], axis=0
                ).T
                term = dot(block[:, :RANK], up_t[...])
                drain(vbuf.at[rows(s)], vsem.at[s])
                value = vbuf[rows(s), :]
                v_aug[rows(s), :HD] = value
                svd[rows(s + 1), :HD] = (value.astype(F32) + term).astype(BF16)
                svd[rows(s + 1), HD:] = block

        @pl.loop(done(g), done(g + 1))
        def _(j):
            slabs = [student_slab(4 * j + at) for at in range(4)]
            seen = [dot(svd[rows(s + 1), HD:], expand[...]) for s in slabs]
            raw = [dot(qbuf[rows(s), :], keys_t[:, rows(s, 3 * TOK)]) for s in slabs]
            raw = [jnp.where(m > 0.5, r, -1e30) for m, r in zip(seen, raw)]
            most = [jnp.max(r, axis=1, keepdims=True) for r in raw]
            expo = [jnp.exp2((r - m) * EXP2_SCALE) for r, m in zip(raw, most)]
            norm = [1.0 / jnp.sum(e, axis=1, keepdims=True) for e in expo]
            weights = [(e * n).astype(BF16) for e, n in zip(expo, norm)]
            mixed = [dot(w, svd[rows(s, 3 * TOK), :]) for w, s in zip(weights, slabs)]
            for s, w, m in zip(slabs, weights, mixed):
                wts[s] = w
                stu[rows(s), :] = m[:, :HD]
                obuf[rows(s), :] = m[:, :HD].astype(BF16)
                mixd[rows(s), :] = m[:, HD:].astype(BF16)

            @pl.when(j > done(g))
            def _():
                send_out(j - 1)

        firsts = [(yy * NZ + place) * 2 for yy in range(2)]

        def score(i, scores, tops):
            block = pl.ds(pl.multiple_of(i * BQ, BQ), BQ)
            query = qbuf[block, :]
            top = high[block, :]
            for yy, first in enumerate(firsts):
                chunk = dot(query, keys_t[:, rows(first + 1, 2 * TOK)])
                scores[:, yy * 2 * TOK : (yy + 1) * 2 * TOK] = chunk
                top = jnp.maximum(top, jnp.maximum(chunk[:, :HD], chunk[:, HD:]))
            tops[...] = jnp.broadcast_to(jnp.max(top, axis=1, keepdims=True), (BQ, HD))

        def update(i, scores, tops):
            block = pl.ds(pl.multiple_of(i * BQ, BQ), BQ)
            new = tops[...]
            alpha = jnp.exp2((high[block, :] - new) * EXP2_SCALE)
            high[block, :] = new
            part = None
            for yy, first in enumerate(firsts):
                expo = jnp.concatenate(
                    [
                        jnp.exp2(
                            (scores[:, (2 * yy + h) * HD : (2 * yy + h + 1) * HD] - new)
                            * EXP2_SCALE
                        ).astype(BF16)
                        for h in range(2)
                    ],
                    axis=1,
                )
                term = dot(expo, v_aug[rows(first, 2 * TOK), :])
                part = term if part is None else part + term
            acc[block, :HD] = acc[block, :HD] * alpha + part[:, :HD]
            acc[block, HD:] = acc[block, HD:] * alpha + part[:, HD:]

        blocks = TOKENS // BQ
        score(0, scores0, tops0)

        @pl.when(done(g + 1) > done(g))
        def _():
            send_out(done(g + 1) - 1)


        @pl.loop(0, blocks // 2 - 1)
        def _(i):
            update(2 * i, scores0, tops0)
            score(2 * i + 1, scores1, tops1)
            update(2 * i + 1, scores1, tops1)
            score(2 * i + 2, scores0, tops0)

        update(blocks - 2, scores0, tops0)
        score(blocks - 1, scores1, tops1)
        update(blocks - 1, scores1, tops1)

    def block(src, offset, owner):
        return src[:, pl.ds(pl.multiple_of(offset + owner * TOK, TOK), TOK)]

    def exchange(k, src, offset, ch):
        for m in range(4):
            owner = 4 * ch + m
            rs_s1[k, owner] = block(src, offset, 2 * owner + 1 - c).astype(BF16)
        part = pl.ds(4 * ch, 4)
        remote(
            rs_s1.at[k, part], rs_r1.at[k, part], rs_sem.at[k, 0], rs_pair.at[k, ch], me + 1 - 2 * c
        ).start()

    def chip_at(i):
        r = N // 2 - 1 - i
        return lax.rem(y + lax.rem(r, 2), 2) * NZ + lax.rem(z + ring_step(r // 2), NZ)

    def scatter(k, src, offset):
        @pl.loop(0, 4)
        def _(ch):
            drain(rs_r1.at[k, pl.ds(4 * ch, 4)], rs_pair.at[k, ch])
            for m in range(4):
                owner = 4 * ch + m
                rs_s2[k, owner] = (
                    block(src, offset, 2 * owner + c) + rs_r1[k, owner].astype(F32)
                ).astype(BF16)

        @pl.loop(0, N // 2 - 1)
        def _(i):
            owner = chip_at(i)
            remote(
                rs_s2.at[k, owner], rs_r2.at[k, chip], rs_sem.at[k, 1], rs_sem.at[k, 2], 2 * owner + c
            ).start()

        rs_r2[k, chip] = rs_s2[k, chip]

    def total(k):
        drain(rs_r2.at[k, pl.ds(0, N // 2 - 1)], rs_sem.at[k, 2])
        result = rs_r2[k, 0].astype(F32)
        for m in range(1, N // 2):
            result = result + rs_r2[k, m].astype(F32)
        return result

    @pl.loop(0, 4)
    def _(ch):
        @pl.loop(0, 2)
        def _(h):
            slabs = [8 * ch + 4 * h + u for u in range(4)]
            span = rows(slabs[0], 4 * TOK)
            teacher = (acc[span, :HD] / acc[span, HD:]).astype(BF16).astype(F32)
            grad = ((stu[span, :] - teacher) * (TOKENS**-0.5)).astype(BF16)
            latent = dot_tt(up_t[...], grad, ((1,), (1,))).astype(BF16)
            terms = [dot(latent[:, u * TOK : (u + 1) * TOK], wts[s]) for u, s in enumerate(slabs)]
            for s, term in zip(slabs, terms):
                hid[:, rows(s, 3 * TOK)] += term
            gup_ref[...] += dot_tt(mixd[span, :RANK], grad, ((0,), (0,)))

        @pl.when(ch > 0)
        def _():
            exchange(0, hid, PAD, ch - 1)

    exchange(0, hid, PAD, 3)


    scatter(0, hid, PAD)

    hidden = total(0)
    hid_hi[...] = hidden.astype(BF16)
    hid_lo[...] = (hidden - hidden.astype(BF16).astype(F32)).astype(BF16)

    def forward(n):
        drain(rs_r1.at[1, pl.ds(4 * n, 4)], rs_pair.at[1, n])
        for u in range(4):
            i = 4 * n + u
            rs_s2[1, i] = (block(gdn, 0, 2 * i + c) + rs_r1[1, i].astype(F32)).astype(BF16)
        for u in range(4):
            i = 4 * n + u

            @pl.when(i < N // 2 - 1)
            def _():
                remote(
                    rs_s2.at[1, i],
                    rs_r2.at[1, i],
                    rs_sem.at[1, 1],
                    rs_sem.at[1, 2],
                    2 * chip_at(i) + c,
                ).start()

    @pl.loop(0, 4)
    def _(n):
        for u in range(4):
            i = 4 * n + u
            feed = xbuf[:, rows(2 * chip_at(i), 2 * TOK)]
            gdn[:, rows(2 * i, 2 * TOK)] = dot(hid_hi[...], feed) + dot(hid_lo[...], feed)
        exchange(1, gdn, 0, n)

        @pl.when(n > 0)
        def _():
            forward(n - 1)

    forward(3)
    rs_r2[1, N // 2 - 1] = rs_s2[1, N // 2 - 1]
    gdown_ref[...] = total(1)

    for a in range(3):
        drain(kbuf.at[pl.ds(0, (N - 1) * TOK)], ssem.at[a])
    drain(dbuf.at[0, pl.ds(0, NZ - 1)], dsem_s.at[0])
    drain(dbuf.at[pl.ds(0, 3)], dsem_s.at[1])
    for k in range(2):
        drain(rs_s1.at[k], rs_sem.at[k, 0])
        drain(rs_s2.at[k, pl.ds(0, N // 2 - 1)], rs_sem.at[k, 1])
    drain(obuf.at[pl.ds(0, (N - 1) * TOK)], osem.at[0])
    drain(obuf.at[pl.ds(0, (N - 1) * TOK)], osem.at[1])
    drain(obuf.at[pl.ds(0, TOK)], osem.at[2])


def local(
    queries, keys, values, value_layer_input, adapter_down_weight, adapter_up_weight, neighbors
):
    anywhere = pl.BlockSpec(memory_space=pl.ANY)
    vmem = pl.BlockSpec(memory_space=pltpu.VMEM)
    dma = pltpu.SemaphoreType.DMA
    student_out, grad_down, grad_up = pl.pallas_call(
        kernel,
        out_shape=(
            pltpu.VMEM((TOK, WIDTH), BF16),
            pltpu.VMEM((RANK, HD), F32),
            pltpu.VMEM((RANK, HD), F32),
        ),
        in_specs=[anywhere] * 6 + [pl.BlockSpec(memory_space=pltpu.SMEM)],
        out_specs=(vmem, vmem, vmem),
        scratch_shapes=[
            pltpu.VMEM((TOK, WIDTH), BF16),
            pltpu.VMEM((RANK, WIDTH), BF16),
            pltpu.VMEM((RANK, HD), BF16),
            pltpu.VMEM((TOKENS, HD), BF16),
            pltpu.VMEM((TOKENS, HD), BF16),
            pltpu.VMEM((TOKENS, HD), BF16),
            pltpu.VMEM((HD, TOKENS + 2 * PAD), BF16),
            pltpu.VMEM((TOKENS, 2 * HD), BF16),
            pltpu.VMEM((TOKENS + 2 * PAD, 2 * HD), BF16),
            pltpu.VMEM((TOK, 3 * TOK), BF16),
            pltpu.VMEM((BQ, CK), F32),
            pltpu.VMEM((BQ, CK), F32),
            pltpu.VMEM((BQ, HD), F32),
            pltpu.VMEM((BQ, HD), F32),
            pltpu.VMEM((TOKENS, HD), F32),
            pltpu.VMEM((TOKENS, 2 * HD), F32),
            pltpu.VMEM((N, TOK, 3 * TOK), BF16),
            pltpu.VMEM((TOKENS, HD), F32),
            pltpu.VMEM((TOKENS, HD), BF16),
            pltpu.VMEM((TOKENS, HD), BF16),
            pltpu.VMEM((4, NZ, DROWS, TOK), BF16),
            pltpu.VMEM((RANK, TOKENS + 2 * PAD), F32),
            pltpu.VMEM((RANK, WIDTH), F32),
            pltpu.VMEM((RANK, TOK), BF16),
            pltpu.VMEM((RANK, TOK), BF16),
            pltpu.VMEM((2, N // 2, RANK, TOK), BF16),
            pltpu.VMEM((2, N // 2, RANK, TOK), BF16),
            pltpu.VMEM((2, N // 2, RANK, TOK), BF16),
            pltpu.VMEM((2, N // 2, RANK, TOK), BF16),
            dma((3,)),
            dma((3,)),
            dma((N,)),
            dma((N,)),
            dma((N,)),
            dma((3,)),
            dma((2,)),
            dma,
            dma((4,)),
            dma((2, 3)),
            dma((2, 4)),
        ],
        compiler_params=pltpu.CompilerParams(
            collective_id=0, has_side_effects=True, vmem_limit_bytes=60 << 20
        ),
    )(
        queries,
        keys,
        values,
        value_layer_input,
        adapter_down_weight.T,
        adapter_up_weight.T,
        neighbors,
    )
    return student_out, grad_down.T, grad_up.T


def solution(mesh):
    rows_split = P(("video", "context"), None)
    return jax.shard_map(
        local,
        mesh=mesh,
        in_specs=(rows_split,) * 4 + (P(), P(), rows_split),
        out_specs=(rows_split,) * 3,
        check_vma=False,
    )
```
